128 devices in a mesh: filt: 8 (over z, x_hi), space: 16 (over x_lo, y, core).
Axes of the slice: x: 4 (x_hi: 2, x_lo: 2; x = x_hi * 2 + x_lo), y: 4, z: 4, core: 2. Of those that a mesh axis runs over, the one named last changes fastest.
Arguments:
- inputs: bfloat16 [16, 256, 2048], P('space', 'filt'), may hold values from -6 to 6
- weight: bfloat16 [3, 3, 3, 256, 256], P(None, None, None, 'filt'), may hold values from -0.078125 to 0.078125
- bias: bfloat16 [256], P('filt'), may hold values from -4 to 4
- cotangent: bfloat16 [16, 256, 2048], P('space', 'filt'), may hold values from -6 to 6
Outputs:
- output: float32 [16, 256, 2048], P('space', 'filt')
- grad_inputs: float32 [16, 256, 2048], P('space', 'filt')
- grad_weight: float32 [3, 3, 3, 256, 256], P(None, None, None, 'filt')
- grad_bias: float32 [256], P('filt')
The draws below stay inside these ranges and needn't reach their ends.
All inputs are finite; a program needn't handle non-finite values.
Results may differ from the reference program's by a relative error of at most 0.0003.
Values may be sent and summed in bfloat16 or wider, within the bound.
No kernel may reach another device: no remote copies, remote signals or barrier semaphores. Data moves between devices by JAX's collectives and lax.ppermute only.
A program may use at most 64 MiB of HBM per device.

```python
import jax
import jax.numpy as jnp
from jax import lax

C = 256
ROWS = 32
WIDE = 64
DEPTH = 16
PLANE = 2048


def block_levels(stream_key, shape, pieces, low, high):
    loudness = 1.0
    for position, blocks in pieces:
        heights = jax.random.uniform(jax.random.fold_in(jax.random.fold_in(stream_key, 6), position), (blocks,), jnp.float32, low / len(pieces), high / len(pieces))
        loudness = loudness * jnp.repeat(jnp.exp(heights), shape[position] // blocks).reshape((-1,) + (1,) * (len(shape) - 1 - position))
    return loudness


def gaussian(key, shape, width, most, pieces=(), kind=jnp.bfloat16):
    values = width * jax.random.normal(key, shape, jnp.float32)
    if pieces:
        values = values * block_levels(key, shape, pieces, -0.22, 0.18)
    return jnp.clip(values, -most, most).astype(kind)


def setup_inputs(seed: int = 0) -> dict:
    streams_of = jax.random.split(jax.random.key(seed), 5)
    inputs = gaussian(streams_of[0], (DEPTH, C, PLANE), 1.0, 6.0, ((0, 16), (1, 8)))
    weight = gaussian(streams_of[1], (3, 3, 3, C, C), (27 * C) ** -0.5, 0.078125, ((3, 8),))
    bias = gaussian(streams_of[2], (C,), 1.0, 4.0, ((0, 8),))
    cotangent = gaussian(streams_of[3], (DEPTH, C, PLANE), 1.0, 6.0, ((0, 16), (1, 8)))
    return dict(inputs=inputs, weight=weight, bias=bias, cotangent=cotangent)


def convolve(volume, kernel):
    result = lax.conv_general_dilated(volume[None], kernel, (1, 1, 1), [(1, 1), (1, 1), (1, 1)], dimension_numbers=('NDCHW', 'DHWIO', 'NDCHW'), precision=lax.Precision.HIGHEST)
    return result[0]

def reference(inputs, weight, bias, cotangent):
    inputs_wide = inputs.astype(jnp.float32).reshape(DEPTH, C, ROWS, WIDE)
    weight_wide = weight.astype(jnp.float32)
    summed, pullback = jax.vjp(convolve, inputs_wide, weight_wide)
    output = summed + bias.astype(jnp.float32)[None, :, None, None]
    grad_wide = cotangent.astype(jnp.float32).reshape(DEPTH, C, ROWS, WIDE)
    grad_in, grad_kernel = pullback(grad_wide)
    factor = 1.0 / jnp.sqrt(jnp.float32(DEPTH * ROWS * WIDE))
    grad_bias = lax.optimization_barrier(jnp.sum(grad_wide, axis=(0, 2, 3))) * factor
    output = output.reshape(DEPTH, C, ROWS * WIDE)
    grad_in = grad_in.reshape(DEPTH, C, ROWS * WIDE)
    return (output, grad_in, grad_kernel * factor, grad_bias)
```

```python
import jax
import jax.numpy as jnp
from jax import lax
from jax.experimental import pallas as pl
from jax.experimental.pallas import tpu as pltpu
from jax.sharding import PartitionSpec as P

ROWS = 32
WIDE = 64
PLANE = ROWS * WIDE
OWN = 32
TAPS = 9 * OWN
HALF = 896
PIECE = HALF // 8
BF = jnp.bfloat16
F32 = jnp.float32

VM = pl.BlockSpec(memory_space=pltpu.VMEM)
PARAMS = pltpu.CompilerParams(vmem_limit_bytes=48 * 1024 * 1024)


def along_z(step):
    return [(f, ((f // 2 + step) % 4) * 2 + f % 2) for f in range(8)]


ACROSS = [(f, f ^ 1) for f in range(8)]
UP = [(s, (s + 1) % 16) for s in range(16)]
DOWN = [((s + 1) % 16, s) for s in range(16)]
CORE = [(s, s ^ 1) for s in range(16)]
XLO = [(s, s ^ 8) for s in range(16)]


def along_y(step):
    return [(s, (s & 9) | ((((s >> 1) + step) & 3) << 1)) for s in range(16)]


def swapped(flip):
    pairs = []
    for f in range(8):
        for s in range(16):
            if s & 1:
                pairs.append((f * 16 + s, (f ^ 1) * 16 + (s ^ flip)))
            else:
                pairs.append((f * 16 + s, f * 16 + (s ^ 8)))
    return pairs


def columns(shape):
    return lax.broadcasted_iota(jnp.int32, shape, 1) & (WIDE - 1)


def lanes(shape):
    return lax.broadcasted_iota(jnp.int32, shape, 1)


def select_kernel(w_ref, mine_ref, theirs_ref):
    filt = lax.axis_index("filt")
    z, xh = filt // 2, filt % 2
    src = lax.broadcasted_iota(jnp.int32, (256, 256), 0)
    lane = lax.broadcasted_iota(jnp.int32, (256, 256), 1)
    side, turn, chan = lane >> 7, (lane >> 5) & 3, lane & 31
    want = ((z + turn) & 3) * 64 + ((xh + side) & 1) * 32 + chan
    pick = jnp.where(src == want, 1.0, 0.0).astype(BF)
    got = jnp.dot(w_ref[...], pick, preferred_element_type=F32).astype(BF)
    mine_ref[...] = got[:, :128]
    theirs_ref[...] = got[:, 128:]


def forward_kernel(prev_ref, here_ref, next_ref, wa_ref, wb_ref, xs_ref, o0, o1, o2, o3):
    space = lax.axis_index("space")
    col = columns((64, PLANE))
    has_prev = (space > 0).astype(F32)
    has_next = (space < 15).astype(F32)
    for kd, ref in enumerate((prev_ref, here_ref, next_ref)):
        wide = ref[...].astype(F32)
        if kd == 0:
            wide = wide * has_prev
        if kd == 2:
            wide = wide * has_next
        left = jnp.where(col == 0, 0.0, pltpu.roll(wide, 1, 1))
        right = jnp.where(col == WIDE - 1, 0.0, pltpu.roll(wide, PLANE - 1, 1))
        for kw, part in enumerate((left, wide, right)):
            at = (kd * 3 + kw) * OWN
            narrow = part.astype(BF)
            xs_ref[0, at : at + OWN, :] = narrow[:OWN]
            xs_ref[1, at : at + OWN, :] = narrow[OWN:]
    xs_ref[:, TAPS:, :] = jnp.ones((2, 16, PLANE), BF)
    rhs = jnp.concatenate([xs_ref[0, :TAPS, :], xs_ref[1, :TAPS, :]], axis=0)
    parts = []
    for kh in range(3):
        lhs = jnp.concatenate(
            [w[(kd * 3 + kh) * 96 : (kd * 3 + kh) * 96 + 96, :] for w in (wa_ref, wb_ref) for kd in range(3)],
            axis=0,
        )
        parts.append(
            lax.dot_general(lhs, rhs, (((0,), (0,)), ((), ())), preferred_element_type=F32)
        )
    lane = lanes((128, PLANE))
    total = (
        parts[1]
        + jnp.where(lane < WIDE, 0.0, pltpu.roll(parts[0], WIDE, 1))
        + jnp.where(lane >= PLANE - WIDE, 0.0, pltpu.roll(parts[2], PLANE - WIDE, 1))
    )
    for r, ref in enumerate((o0, o1, o2, o3)):
        ref[...] = total[r * 32 : r * 32 + 32]


def row_shifts(wide):
    lane = lanes(wide.shape)
    turned = pltpu.roll(wide, PLANE - WIDE, 1)
    up = jnp.where(lane >= PLANE - WIDE, 0.0, turned)
    down = jnp.where(lane < WIDE, 0.0, pltpu.roll(wide, WIDE, 1))
    return up.astype(BF), wide.astype(BF), down.astype(BF)


def kernel_grad_kernel(xs_ref, c0, c1, c2, c3, keep_ref, send_ref, cs_ref):
    core = lax.axis_index("space") & 1
    for r, ref in enumerate((c0, c1, c2, c3)):
        for kh, part in enumerate(row_shifts(ref[...].astype(F32))):
            cs_ref[kh * 128 + r * 32 : kh * 128 + r * 32 + 32, :] = part
    for slot, ref in enumerate((keep_ref, send_ref)):
        got = lax.dot_general(
            xs_ref[core ^ slot], cs_ref[...], (((1,), (1,)), ((), ())), preferred_element_type=F32
        )
        for kh in range(3):
            ref[kh * TAPS : (kh + 1) * TAPS, :] = got[:TAPS, kh * 128 : kh * 128 + 128]
        ref[3 * TAPS : 3 * TAPS + 16, :] = got[TAPS:, 128:256]
        ref[3 * TAPS + 16 :, :] = got[TAPS:, 128:256]


def input_grad_kernel(prev_ref, next_ref, c0, c1, c2, c3, wa_ref, wb_ref, mine_ref, theirs_ref, cs_ref):
    space = lax.axis_index("space")
    has_prev = (space > 0).astype(F32)
    has_next = (space < 15).astype(F32)
    for r, ref in enumerate((c0, c1, c2, c3)):
        rows = slice(r * 32, r * 32 + 32)
        planes = (
            next_ref[rows, :].astype(F32) * has_next,
            ref[...].astype(F32),
            prev_ref[rows, :].astype(F32) * has_prev,
        )
        for kd, wide in enumerate(planes):
            for kh, part in enumerate(row_shifts(wide)):
                at = (kd * 3 + kh) * 128 + r * 32
                cs_ref[at : at + 32, :] = part
    lhs = jnp.concatenate(
        [
            jnp.concatenate([w[t * 96 : t * 96 + 96, :] for t in range(9)], axis=1)
            for w in (wa_ref, wb_ref)
        ],
        axis=0,
    )
    got = jnp.dot(lhs, cs_ref[...], preferred_element_type=F32)
    col = columns((OWN, PLANE))
    for h, ref in enumerate((mine_ref, theirs_ref)):
        base = h * 96
        ref[...] = (
            got[base + 32 : base + 64]
            + jnp.where(col == WIDE - 1, 0.0, pltpu.roll(got[base : base + 32], PLANE - 1, 1))
            + jnp.where(col == 0, 0.0, pltpu.roll(got[base + 64 : base + 96], 1, 1))
        )


def assemble_kernel(own_ref, other_ref, grad_ref, bias_ref, both_ref, *, factor):
    filt, space = lax.axis_index("filt"), lax.axis_index("space")
    z, xh = filt // 2, filt % 2
    xlo, y, core = space // 8, (space // 2) & 3, space & 1
    for side, ref in enumerate((own_ref, other_ref)):
        for ry in range(4):
            for rx in range(2):
                at = (ry * 2 + rx) * PIECE
                to = pl.multiple_of(((xlo ^ rx) * 4 + ((y + ry) & 3)) * PIECE, 8)
                both_ref[pl.ds(to, PIECE), side * 128 : side * 128 + 128] = ref[at : at + PIECE, :]
    src = lax.broadcasted_iota(jnp.int32, (256, 256), 0)
    lane = lax.broadcasted_iota(jnp.int32, (256, 256), 1)
    side, turn, chan = src >> 7, (src >> 5) & 3, src & 31
    want = ((z + turn) & 3) * 64 + ((xh + core + side) & 1) * 32 + chan
    pick = jnp.where(lane == want, 1.0, 0.0)
    got = jnp.dot(both_ref[: 3 * TAPS, :], pick, precision=lax.Precision.HIGHEST, preferred_element_type=F32)
    got = got * factor
    for kd in range(3):
        for kh in range(3):
            grad_ref[(kd * 3 + kh) * 96 : (kd * 3 + kh) * 96 + 96, :] = got[
                kh * TAPS + kd * 96 : kh * TAPS + kd * 96 + 96
            ]
    tail = both_ref[3 * TAPS : 3 * TAPS + 8, :]
    bias_ref[...] = jnp.where(core == 0, tail[:, :128], tail[:, 128:]) * factor


def call(kernel, outs, *args, scratch=()):
    return pl.pallas_call(
        kernel,
        out_shape=[jax.ShapeDtypeStruct(s, d) for s, d in outs],
        in_specs=[VM] * len(args),
        out_specs=[VM] * len(outs),
        scratch_shapes=list(scratch),
        compiler_params=PARAMS,
    )(*args)


def body(inputs, weight, bias, cotangent):
    space = lax.axis_index("space")
    xlo, y = space // 8, (space // 2) & 3
    x_own = inputs[0]
    c_own = cotangent[0]

    cots = [c_own] + [lax.ppermute(c_own, "filt", along_z(-r)) for r in (1, 2, 3)]
    x_other = lax.ppermute(x_own, "filt", ACROSS)
    w_mine, w_theirs = call(
        select_kernel, [((864, 128), BF), ((864, 128), BF)], weight.reshape(864, 256)
    )
    w_other = lax.ppermute(w_theirs, "filt", ACROSS)

    x_here = jnp.concatenate([x_own, x_other], axis=0)
    x_prev = lax.ppermute(x_here, "space", UP)
    x_next = lax.ppermute(x_here, "space", DOWN)
    c_here = jnp.concatenate(cots, axis=0)
    c_prev = lax.ppermute(c_here, "space", UP)
    c_next = lax.ppermute(c_here, "space", DOWN)

    xs, *outs = call(
        forward_kernel,
        [((2, TAPS + 16, PLANE), BF)] + [((32, PLANE), F32)] * 4,
        x_prev,
        x_here,
        x_next,
        w_mine,
        w_other,
    )
    keep, send = call(
        kernel_grad_kernel,
        [((HALF, 128), F32)] * 2,
        xs,
        *cots,
        scratch=[pltpu.VMEM((384, PLANE), BF)],
    )
    r_core = keep + lax.ppermute(send, "space", CORE)
    half = HALF // 2
    r_send = lax.dynamic_slice_in_dim(r_core, (1 - xlo) * half, half, 0)
    r_keep = lax.dynamic_slice_in_dim(r_core, xlo * half, half, 0)
    r_xlo = r_keep + lax.ppermute(r_send, "space", XLO)

    def part(r):
        return lax.dynamic_slice_in_dim(r_xlo, ((y + r) & 3) * PIECE, PIECE, 0)

    piece = part(0)
    for r in (1, 2, 3):
        piece = piece + lax.ppermute(part(r), "space", along_y(r))

    summed = outs[0]
    for r in (1, 2, 3):
        summed = summed + lax.ppermute(outs[r], "filt", along_z(r))
    output = summed + bias.astype(F32)[:, None]

    g_mine, g_theirs = call(
        input_grad_kernel,
        [((OWN, PLANE), F32)] * 2,
        c_prev,
        c_next,
        *cots,
        w_mine,
        w_other,
        scratch=[pltpu.VMEM((9 * 128, PLANE), BF)],
    )
    grad_inputs = g_mine + lax.ppermute(g_theirs, "filt", ACROSS)

    first = lax.ppermute(piece, ("filt", "space"), swapped(0))
    second = lax.ppermute(piece, ("filt", "space"), swapped(8))
    even = (space & 1) == 0
    pair = jnp.concatenate(
        [jnp.where(even, piece, first), jnp.where(even, first, second)], axis=0
    )
    mine = jnp.concatenate(
        [pair] + [lax.ppermute(pair, "space", along_y(-r)) for r in (1, 2, 3)], axis=0
    )
    other = lax.ppermute(mine, "space", CORE)
    factor = float((16 * PLANE) ** -0.5)
    grad_weight, grad_bias = call(
        lambda *refs: assemble_kernel(*refs, factor=factor),
        [((864, 256), F32), ((8, 128), F32)],
        mine,
        other,
        scratch=[pltpu.VMEM((HALF, 256), F32)],
    )
    return (
        output[None],
        grad_inputs[None],
        grad_weight.reshape(3, 3, 3, OWN, 256),
        grad_bias[0, :OWN],
    )


def solution(mesh):
    placed = (
        P("space", "filt", None),
        P(None, None, None, "filt", None),
        P("filt"),
        P("space", "filt", None),
    )
    return jax.shard_map(
        body,
        mesh=mesh,
        in_specs=placed,
        out_specs=(
            P("space", "filt", None),
            P("space", "filt", None),
            P(None, None, None, "filt", None),
            P("filt"),
        ),
        check_vma=False,
    )
```

```python
import jax
import jax.numpy as jnp
from jax import lax
from jax.experimental import pallas as pl
from jax.experimental.pallas import tpu as pltpu
from jax.sharding import PartitionSpec as P


ROWS = 32
WIDE = 64
PLANE = ROWS * WIDE
OWN = 32
TAPS = 9 * OWN
HALF = 896
PIECE = HALF // 8
BF = jnp.bfloat16
F32 = jnp.float32

VM = pl.BlockSpec(memory_space=pltpu.VMEM)
PARAMS = pltpu.CompilerParams(vmem_limit_bytes=48 * 1024 * 1024)


def along_z(step):
    return [(f, ((f // 2 + step) % 4) * 2 + f % 2) for f in range(8)]


ACROSS = [(f, f ^ 1) for f in range(8)]
UP = [(s, (s + 1) % 16) for s in range(16)]
DOWN = [((s + 1) % 16, s) for s in range(16)]
CORE = [(s, s ^ 1) for s in range(16)]
XLO = [(s, s ^ 8) for s in range(16)]


def along_y(step):
    return [(s, (s & 9) | ((((s >> 1) + step) & 3) << 1)) for s in range(16)]


def swapped(flip):
    pairs = []
    for f in range(8):
        for s in range(16):
            if s & 1:
                pairs.append((f * 16 + s, (f ^ 1) * 16 + (s ^ flip)))
            else:
                pairs.append((f * 16 + s, f * 16 + (s ^ 8)))
    return pairs


def columns(shape):
    return lax.broadcasted_iota(jnp.int32, shape, 1) & (WIDE - 1)


def lanes(shape):
    return lax.broadcasted_iota(jnp.int32, shape, 1)


def select_kernel(w_ref, x_ref, c_ref, mine_ref, theirs_ref, x_out, c_out):
    x_out[...] = x_ref[...]
    c_out[...] = c_ref[...]
    filt = lax.axis_index("filt")
    z, xh = filt // 2, filt % 2
    src = lax.broadcasted_iota(jnp.int32, (256, 256), 0)
    lane = lax.broadcasted_iota(jnp.int32, (256, 256), 1)
    side, turn, chan = lane >> 7, (lane >> 5) & 3, lane & 31
    want = ((z + turn) & 3) * 64 + ((xh + side) & 1) * 32 + chan
    pick = jnp.where(src == want, 1.0, 0.0).astype(BF)
    got = jnp.dot(w_ref[...], pick, preferred_element_type=F32).astype(BF)
    mine_ref[...] = got[:, :128]
    theirs_ref[...] = got[:, 128:]


def join_kernel(*refs):
    *parts, out_ref = refs
    at = 0
    for ref in parts:
        out_ref[at : at + ref.shape[0], :] = ref[...]
        at += ref.shape[0]


def forward_kernel(xs_ref, wa_ref, wb_ref, o0, o1, o2, o3):
    rhs = jnp.concatenate([xs_ref[0, :TAPS, :], xs_ref[1, :TAPS, :]], axis=0)
    parts = []
    for kh in range(3):
        lhs = jnp.concatenate(
            [w[(kd * 3 + kh) * 96 : (kd * 3 + kh) * 96 + 96, :] for w in (wa_ref, wb_ref) for kd in range(3)],
            axis=0,
        )
        parts.append(
            lax.dot_general(lhs, rhs, (((0,), (0,)), ((), ())), preferred_element_type=F32)
        )
    lane = lanes((128, PLANE))
    total = (
        parts[1]
        + jnp.where(lane < WIDE, 0.0, pltpu.roll(parts[0], WIDE, 1))
        + jnp.where(lane >= PLANE - WIDE, 0.0, pltpu.roll(parts[2], PLANE - WIDE, 1))
    )
    for r, ref in enumerate((o0, o1, o2, o3)):
        ref[...] = total[r * 32 : r * 32 + 32]


def row_shifts(wide):
    lane = lanes(wide.shape)
    turned = pltpu.roll(wide, PLANE - WIDE, 1)
    up = jnp.where(lane >= PLANE - WIDE, 0.0, turned)
    down = jnp.where(lane < WIDE, 0.0, pltpu.roll(wide, WIDE, 1))
    return up.astype(BF), wide.astype(BF), down.astype(BF)


def kernel_grad_kernel(prev_ref, here_ref, next_ref, c0, c1, c2, c3, xs_ref, keep_ref, send_ref, cs_ref):
    space = lax.axis_index("space")
    core = space & 1
    col = columns((64, PLANE))
    has_prev = (space > 0).astype(F32)
    has_next = (space < 15).astype(F32)
    for kd, ref in enumerate((prev_ref, here_ref, next_ref)):
        wide = ref[...].astype(F32)
        if kd == 0:
            wide = wide * has_prev
        if kd == 2:
            wide = wide * has_next
        left = jnp.where(col == 0, 0.0, pltpu.roll(wide, 1, 1))
        right = jnp.where(col == WIDE - 1, 0.0, pltpu.roll(wide, PLANE - 1, 1))
        for kw, part in enumerate((left, wide, right)):
            at = (kd * 3 + kw) * OWN
            narrow = part.astype(BF)
            xs_ref[0, at : at + OWN, :] = narrow[:OWN]
            xs_ref[1, at : at + OWN, :] = narrow[OWN:]
    xs_ref[:, TAPS:, :] = jnp.ones((2, 16, PLANE), BF)
    for r, ref in enumerate((c0, c1, c2, c3)):
        for kh, part in enumerate(row_shifts(ref[...].astype(F32))):
            cs_ref[kh * 128 + r * 32 : kh * 128 + r * 32 + 32, :] = part
    for slot, ref in enumerate((keep_ref, send_ref)):
        got = lax.dot_general(
            xs_ref[core ^ slot], cs_ref[...], (((1,), (1,)), ((), ())), preferred_element_type=F32
        )
        for kh in range(3):
            ref[kh * TAPS : (kh + 1) * TAPS, :] = got[:TAPS, kh * 128 : kh * 128 + 128]
        ref[3 * TAPS : 3 * TAPS + 16, :] = got[TAPS:, 128:256]
        ref[3 * TAPS + 16 :, :] = got[TAPS:, 128:256]


def input_grad_kernel(prev_ref, next_ref, c0, c1, c2, c3, wa_ref, wb_ref, mine_ref, theirs_ref, cs_ref):
    space = lax.axis_index("space")
    has_prev = (space > 0).astype(F32)
    has_next = (space < 15).astype(F32)
    for r, ref in enumerate((c0, c1, c2, c3)):
        rows = slice(r * 32, r * 32 + 32)
        planes = (
            next_ref[rows, :].astype(F32) * has_next,
            ref[...].astype(F32),
            prev_ref[rows, :].astype(F32) * has_prev,
        )
        for kd, wide in enumerate(planes):
            for kh, part in enumerate(row_shifts(wide)):
                at = (kd * 3 + kh) * 128 + r * 32
                cs_ref[at : at + 32, :] = part
    lhs = jnp.concatenate(
        [
            jnp.concatenate([w[t * 96 : t * 96 + 96, :] for t in range(9)], axis=1)
            for w in (wa_ref, wb_ref)
        ],
        axis=0,
    )
    got = jnp.dot(lhs, cs_ref[...], preferred_element_type=F32)
    col = columns((OWN, PLANE))
    for h, ref in enumerate((mine_ref, theirs_ref)):
        base = h * 96
        ref[...] = (
            got[base + 32 : base + 64]
            + jnp.where(col == WIDE - 1, 0.0, pltpu.roll(got[base : base + 32], PLANE - 1, 1))
            + jnp.where(col == 0, 0.0, pltpu.roll(got[base + 64 : base + 96], 1, 1))
        )


def assemble_kernel(own_ref, other_ref, grad_ref, bias_ref, both_ref, *, factor):
    filt, space = lax.axis_index("filt"), lax.axis_index("space")
    z, xh = filt // 2, filt % 2
    xlo, y, core = space // 8, (space // 2) & 3, space & 1
    for side, ref in enumerate((own_ref, other_ref)):
        for ry in range(4):
            for rx in range(2):
                at = (ry * 2 + rx) * PIECE
                to = pl.multiple_of(((xlo ^ rx) * 4 + ((y + ry) & 3)) * PIECE, 8)
                both_ref[pl.ds(to, PIECE), side * 128 : side * 128 + 128] = ref[at : at + PIECE, :]
    src = lax.broadcasted_iota(jnp.int32, (256, 256), 0)
    lane = lax.broadcasted_iota(jnp.int32, (256, 256), 1)
    side, turn, chan = src >> 7, (src >> 5) & 3, src & 31
    want = ((z + turn) & 3) * 64 + ((xh + core + side) & 1) * 32 + chan
    pick = jnp.where(lane == want, 1.0, 0.0)
    got = jnp.dot(both_ref[: 3 * TAPS, :], pick, precision=lax.Precision.HIGHEST, preferred_element_type=F32)
    got = got * factor
    for kd in range(3):
        for kh in range(3):
            grad_ref[(kd * 3 + kh) * 96 : (kd * 3 + kh) * 96 + 96, :] = got[
                kh * TAPS + kd * 96 : kh * TAPS + kd * 96 + 96
            ]
    tail = both_ref[3 * TAPS : 3 * TAPS + 1, :]
    bias_ref[...] = jnp.where(core == 0, tail[:, :OWN], tail[:, 128 : 128 + OWN]) * factor


def split_xlo_kernel(keep_ref, got_ref, send_out, keep_out):
    half = HALF // 2
    xlo = lax.axis_index("space") // 8
    for out, at in ((send_out, (1 - xlo) * half), (keep_out, xlo * half)):
        rows = pl.ds(pl.multiple_of(at, 8), half)
        out[...] = keep_ref[rows, :] + got_ref[rows, :]


def split_y_kernel(keep_ref, got_ref, *outs):
    y = (lax.axis_index("space") // 2) & 3
    for r, out in enumerate(outs):
        rows = pl.ds(pl.multiple_of(((y + r) & 3) * PIECE, 8), PIECE)
        out[...] = keep_ref[rows, :] + got_ref[rows, :]


def add4_kernel(a, b, c, d, out):
    out[...] = (a[...] + b[...]) + (c[...] + d[...])


def pair_kernel(piece_ref, first_ref, second_ref, out_ref):
    even = (lax.axis_index("space") & 1) == 0
    out_ref[:PIECE, :] = jnp.where(even, piece_ref[...], first_ref[...])
    out_ref[PIECE:, :] = jnp.where(even, first_ref[...], second_ref[...])


def call(kernel, outs, *args, scratch=()):
    return pl.pallas_call(
        kernel,
        out_shape=[jax.ShapeDtypeStruct(s, d) for s, d in outs],
        in_specs=[VM] * len(args),
        out_specs=[VM] * len(outs),
        scratch_shapes=list(scratch),
        compiler_params=PARAMS,
    )(*args)


def step(inputs, weight, bias, cotangent):
    x_own = inputs[0]
    c_own = cotangent[0]

    x_other = lax.ppermute(x_own, "filt", ACROSS)
    c1, c3, c2 = (lax.ppermute(c_own, "filt", along_z(-r)) for r in (1, 3, 2))
    w_mine, w_theirs, x_near, c_near = call(
        select_kernel,
        [((864, 128), BF), ((864, 128), BF), ((OWN, PLANE), BF), ((OWN, PLANE), BF)],
        weight.reshape(864, 256),
        x_own,
        c_own,
    )
    w_other = lax.ppermute(w_theirs, "filt", ACROSS)
    cots = [c_near, c1, c2, c3]

    (x_here,) = call(join_kernel, [((64, PLANE), BF)], x_near, x_other)
    x_prev = lax.ppermute(x_here, "space", UP)
    x_next = lax.ppermute(x_here, "space", DOWN)

    xs, keep, send = call(
        kernel_grad_kernel,
        [((2, TAPS + 16, PLANE), BF)] + [((HALF, 128), F32)] * 2,
        x_prev,
        x_here,
        x_next,
        *cots,
        scratch=[pltpu.VMEM((384, PLANE), BF)],
    )
    r_core = lax.ppermute(send, "space", CORE)
    outs = call(forward_kernel, [((32, PLANE), F32)] * 4, xs, w_mine, w_other)
    (c_here,) = call(join_kernel, [((128, PLANE), BF)], *cots)

    half = HALF // 2
    r_send, r_keep = call(split_xlo_kernel, [((half, 128), F32)] * 2, keep, r_core)
    r_xlo = lax.ppermute(r_send, "space", XLO)
    c_prev = lax.ppermute(c_here, "space", UP)
    c_next = lax.ppermute(c_here, "space", DOWN)

    parts = call(split_y_kernel, [((PIECE, 128), F32)] * 4, r_keep, r_xlo)
    got = [lax.ppermute(parts[r], "space", along_y(r)) for r in (1, 3, 2)]
    (piece,) = call(add4_kernel, [((PIECE, 128), F32)], parts[0], *got)

    summed = outs[0]
    for r in (1, 3, 2):
        summed = summed + lax.ppermute(outs[r], "filt", along_z(r))
    output = summed + bias.astype(F32)[:, None]

    first = lax.ppermute(piece, ("filt", "space"), swapped(0))
    second = lax.ppermute(piece, ("filt", "space"), swapped(8))
    g_mine, g_theirs = call(
        input_grad_kernel,
        [((OWN, PLANE), F32)] * 2,
        c_prev,
        c_next,
        *cots,
        w_mine,
        w_other,
        scratch=[pltpu.VMEM((9 * 128, PLANE), BF)],
    )
    grad_inputs = g_mine + lax.ppermute(g_theirs, "filt", ACROSS)

    (pair,) = call(pair_kernel, [((2 * PIECE, 128), F32)], piece, first, second)
    turned = {r: lax.ppermute(pair, "space", along_y(-r)) for r in (1, 3, 2)}
    (mine,) = call(join_kernel, [((HALF, 128), F32)], pair, turned[1], turned[2], turned[3])
    other = lax.ppermute(mine, "space", CORE)
    factor = float((16 * PLANE) ** -0.5)
    grad_weight, grad_bias = call(
        lambda *refs: assemble_kernel(*refs, factor=factor),
        [((864, 256), F32), ((1, OWN), F32)],
        mine,
        other,
        scratch=[pltpu.VMEM((HALF, 256), F32)],
    )
    return (
        output[None],
        grad_inputs[None],
        grad_weight.reshape(3, 3, 3, OWN, 256),
        grad_bias.reshape(OWN),
    )


def solution(mesh):
    placed = (
        P("space", "filt", None),
        P(None, None, None, "filt", None),
        P("filt"),
        P("space", "filt", None),
    )
    return jax.shard_map(
        step,
        mesh=mesh,
        in_specs=placed,
        out_specs=(
            P("space", "filt", None),
            P("space", "filt", None),
            P(None, None, None, "filt", None),
            P("filt"),
        ),
        check_vma=False,
    )
```

```python
import jax
import jax.numpy as jnp
from jax import lax
from jax.experimental import pallas as pl
from jax.experimental.pallas import tpu as pltpu
from jax.sharding import PartitionSpec as P


ROWS = 32
WIDE = 64
PLANE = ROWS * WIDE
OWN = 32
TAPS = 9 * OWN
HALF = 896
PIECE = HALF // 8
BF = jnp.bfloat16
F32 = jnp.float32

VM = pl.BlockSpec(memory_space=pltpu.VMEM)
PARAMS = pltpu.CompilerParams(vmem_limit_bytes=48 * 1024 * 1024)


def along_z(step):
    return [(f, ((f // 2 + step) % 4) * 2 + f % 2) for f in range(8)]


ACROSS = [(f, f ^ 1) for f in range(8)]
UP = [(s, (s + 1) % 16) for s in range(16)]
DOWN = [((s + 1) % 16, s) for s in range(16)]
CORE = [(s, s ^ 1) for s in range(16)]
XLO = [(s, s ^ 8) for s in range(16)]


def along_y(step):
    return [(s, (s & 9) | ((((s >> 1) + step) & 3) << 1)) for s in range(16)]


def swapped(flip):
    pairs = []
    for f in range(8):
        for s in range(16):
            if s & 1:
                pairs.append((f * 16 + s, (f ^ 1) * 16 + (s ^ flip)))
            else:
                pairs.append((f * 16 + s, f * 16 + (s ^ 8)))
    return pairs


def columns(shape):
    return lax.broadcasted_iota(jnp.int32, shape, 1) & (WIDE - 1)


def lanes(shape):
    return lax.broadcasted_iota(jnp.int32, shape, 1)


def select_kernel(w_hbm, x_hbm, c_hbm, mine_ref, theirs_ref, x_out, c_out, w_ref, sems):
    copies = [
        pltpu.make_async_copy(a, b, sems.at[i])
        for i, (a, b) in enumerate(((w_hbm, w_ref), (x_hbm, x_out), (c_hbm, c_out)))
    ]
    for copy in copies:
        copy.start()
    filt = lax.axis_index("filt")
    z, xh = filt // 2, filt % 2
    src = lax.broadcasted_iota(jnp.int32, (256, 256), 0)
    lane = lax.broadcasted_iota(jnp.int32, (256, 256), 1)
    side, turn, chan = lane >> 7, (lane >> 5) & 3, lane & 31
    want = ((z + turn) & 3) * 64 + ((xh + side) & 1) * 32 + chan
    pick = jnp.where(src == want, 1.0, 0.0).astype(BF)
    for copy in copies:
        copy.wait()
    got = jnp.dot(w_ref[...], pick, preferred_element_type=F32).astype(BF)
    mine_ref[...] = got[:, :128]
    theirs_ref[...] = got[:, 128:]


def join_kernel(*refs):
    *parts, out_ref = refs
    at = 0
    for ref in parts:
        out_ref[at : at + ref.shape[0], :] = ref[...]
        at += ref.shape[0]


def forward_kernel(xs_ref, wa_ref, wb_ref, o0, o1, o2, o3):
    rhs = jnp.concatenate([xs_ref[0, :TAPS, :], xs_ref[1, :TAPS, :]], axis=0)
    parts = []
    for kh in range(3):
        lhs = jnp.concatenate(
            [w[(kd * 3 + kh) * 96 : (kd * 3 + kh) * 96 + 96, :] for w in (wa_ref, wb_ref) for kd in range(3)],
            axis=0,
        )
        parts.append(
            lax.dot_general(lhs, rhs, (((0,), (0,)), ((), ())), preferred_element_type=F32)
        )
    lane = lanes((128, PLANE))
    total = (
        parts[1]
        + jnp.where(lane < WIDE, 0.0, pltpu.roll(parts[0], WIDE, 1))
        + jnp.where(lane >= PLANE - WIDE, 0.0, pltpu.roll(parts[2], PLANE - WIDE, 1))
    )
    for r, ref in enumerate((o0, o1, o2, o3)):
        ref[...] = total[r * 32 : r * 32 + 32]


def row_shifts(wide):
    lane = lanes(wide.shape)
    turned = pltpu.roll(wide, PLANE - WIDE, 1)
    up = jnp.where(lane >= PLANE - WIDE, 0.0, turned)
    down = jnp.where(lane < WIDE, 0.0, pltpu.roll(wide, WIDE, 1))
    return up.astype(BF), wide.astype(BF), down.astype(BF)


def kernel_grad_kernel(prev_ref, here_ref, next_ref, c0, c1, c2, c3, xs_ref, keep_ref, send_ref, cs_ref):
    space = lax.axis_index("space")
    core = space & 1
    col = columns((64, PLANE))
    has_prev = (space > 0).astype(F32)
    has_next = (space < 15).astype(F32)
    for kd, ref in enumerate((prev_ref, here_ref, next_ref)):
        wide = ref[...].astype(F32)
        if kd == 0:
            wide = wide * has_prev
        if kd == 2:
            wide = wide * has_next
        left = jnp.where(col == 0, 0.0, pltpu.roll(wide, 1, 1))
        right = jnp.where(col == WIDE - 1, 0.0, pltpu.roll(wide, PLANE - 1, 1))
        for kw, part in enumerate((left, wide, right)):
            at = (kd * 3 + kw) * OWN
            narrow = part.astype(BF)
            xs_ref[0, at : at + OWN, :] = narrow[:OWN]
            xs_ref[1, at : at + OWN, :] = narrow[OWN:]
    xs_ref[:, TAPS:, :] = jnp.ones((2, 16, PLANE), BF)
    for r, ref in enumerate((c0, c1, c2, c3)):
        for kh, part in enumerate(row_shifts(ref[...].astype(F32))):
            cs_ref[kh * 128 + r * 32 : kh * 128 + r * 32 + 32, :] = part
    for slot, ref in enumerate((keep_ref, send_ref)):
        got = lax.dot_general(
            xs_ref[core ^ slot], cs_ref[...], (((1,), (1,)), ((), ())), preferred_element_type=F32
        )
        for kh in range(3):
            ref[kh * TAPS : (kh + 1) * TAPS, :] = got[:TAPS, kh * 128 : kh * 128 + 128]
        ref[3 * TAPS : 3 * TAPS + 16, :] = got[TAPS:, 128:256]
        ref[3 * TAPS + 16 :, :] = got[TAPS:, 128:256]


def input_grad_kernel(prev_ref, next_ref, c0, c1, c2, c3, wa_ref, wb_ref, mine_ref, theirs_ref, cs_ref):
    space = lax.axis_index("space")
    has_prev = (space > 0).astype(F32)
    has_next = (space < 15).astype(F32)
    for r, ref in enumerate((c0, c1, c2, c3)):
        rows = slice(r * 32, r * 32 + 32)
        planes = (
            next_ref[rows, :].astype(F32) * has_next,
            ref[...].astype(F32),
            prev_ref[rows, :].astype(F32) * has_prev,
        )
        for kd, wide in enumerate(planes):
            for kh, part in enumerate(row_shifts(wide)):
                at = (kd * 3 + kh) * 128 + r * 32
                cs_ref[at : at + 32, :] = part
    lhs = jnp.concatenate(
        [
            jnp.concatenate([w[t * 96 : t * 96 + 96, :] for t in range(9)], axis=1)
            for w in (wa_ref, wb_ref)
        ],
        axis=0,
    )
    got = jnp.dot(lhs, cs_ref[...], preferred_element_type=F32)
    col = columns((OWN, PLANE))
    for h, ref in enumerate((mine_ref, theirs_ref)):
        base = h * 96
        ref[...] = (
            got[base + 32 : base + 64]
            + jnp.where(col == WIDE - 1, 0.0, pltpu.roll(got[base : base + 32], PLANE - 1, 1))
            + jnp.where(col == 0, 0.0, pltpu.roll(got[base + 64 : base + 96], 1, 1))
        )


def assemble_kernel(own_ref, other_ref, grad_ref, bias_ref, both_ref, *, factor):
    filt, space = lax.axis_index("filt"), lax.axis_index("space")
    z, xh = filt // 2, filt % 2
    xlo, y, core = space // 8, (space // 2) & 3, space & 1
    for side, ref in enumerate((own_ref, other_ref)):
        for ry in range(4):
            for rx in range(2):
                at = (ry * 2 + rx) * PIECE
                to = pl.multiple_of(((xlo ^ rx) * 4 + ((y + ry) & 3)) * PIECE, 8)
                both_ref[pl.ds(to, PIECE), side * 128 : side * 128 + 128] = ref[at : at + PIECE, :]
    src = lax.broadcasted_iota(jnp.int32, (256, 256), 0)
    lane = lax.broadcasted_iota(jnp.int32, (256, 256), 1)
    side, turn, chan = src >> 7, (src >> 5) & 3, src & 31
    want = ((z + turn) & 3) * 64 + ((xh + core + side) & 1) * 32 + chan
    pick = jnp.where(lane == want, 1.0, 0.0).astype(BF)
    left = both_ref[: 3 * TAPS, :] * factor
    got = jnp.zeros(left.shape, F32)
    for _ in range(3):
        part = left.astype(BF)
        left = left - part.astype(F32)
        got = got + jnp.dot(part, pick, preferred_element_type=F32)
    for kd in range(3):
        for kh in range(3):
            grad_ref[(kd * 3 + kh) * 96 : (kd * 3 + kh) * 96 + 96, :] = got[
                kh * TAPS + kd * 96 : kh * TAPS + kd * 96 + 96
            ]
    tail = both_ref[3 * TAPS : 3 * TAPS + 1, :]
    bias_ref[...] = jnp.where(core == 0, tail[:, :OWN], tail[:, 128 : 128 + OWN]) * factor


def split_xlo_kernel(keep_ref, got_ref, send_out, keep_out):
    half = HALF // 2
    xlo = lax.axis_index("space") // 8
    for out, at in ((send_out, (1 - xlo) * half), (keep_out, xlo * half)):
        rows = pl.ds(pl.multiple_of(at, 8), half)
        out[...] = keep_ref[rows, :] + got_ref[rows, :]


def split_y_kernel(keep_ref, got_ref, *outs):
    y = (lax.axis_index("space") // 2) & 3
    for r, out in enumerate(outs):
        rows = pl.ds(pl.multiple_of(((y + r) & 3) * PIECE, 8), PIECE)
        out[...] = keep_ref[rows, :] + got_ref[rows, :]


def bias_kernel(ref, out):
    row = lax.broadcasted_iota(jnp.int32, (OWN, OWN), 0)
    col = lax.broadcasted_iota(jnp.int32, (OWN, OWN), 1)
    wide = jnp.where(row == col, ref[...].astype(F32), 0.0)
    out[...] = jnp.sum(wide, axis=1, keepdims=True)


def output_kernel(a, b, c, d, bias_ref, out):
    out[...] = (a[...] + b[...]) + (c[...] + d[...]) + bias_ref[...]


def add2_kernel(a, b, out):
    out[...] = a[...] + b[...]


def add4_kernel(a, b, c, d, out):
    out[...] = (a[...] + b[...]) + (c[...] + d[...])


def pair_kernel(piece_ref, first_ref, second_ref, out_ref):
    even = (lax.axis_index("space") & 1) == 0
    out_ref[:PIECE, :] = jnp.where(even, piece_ref[...], first_ref[...])
    out_ref[PIECE:, :] = jnp.where(even, first_ref[...], second_ref[...])


def call(kernel, outs, *args, scratch=(), space=VM):
    return pl.pallas_call(
        kernel,
        out_shape=[jax.ShapeDtypeStruct(s, d) for s, d in outs],
        in_specs=[space] * len(args),
        out_specs=[VM] * len(outs),
        scratch_shapes=list(scratch),
        compiler_params=PARAMS,
    )(*args)


def step(inputs, weight, bias, cotangent):
    x_own = inputs[0]
    c_own = cotangent[0]

    x_other = lax.ppermute(x_own, "filt", ACROSS)
    c1, c3, c2 = (lax.ppermute(c_own, "filt", along_z(-r)) for r in (1, 3, 2))
    w_mine, w_theirs, x_near, c_near = call(
        select_kernel,
        [((864, 128), BF), ((864, 128), BF), ((OWN, PLANE), BF), ((OWN, PLANE), BF)],
        *(pltpu.with_memory_space_constraint(v, pltpu.HBM) for v in (weight.reshape(864, 256), x_own, c_own)),
        scratch=[pltpu.VMEM((864, 256), BF), pltpu.SemaphoreType.DMA((3,))],
        space=pl.BlockSpec(memory_space=pltpu.HBM),
    )
    w_other = lax.ppermute(w_theirs, "filt", ACROSS)
    cots = [c_near, c1, c2, c3]

    (x_here,) = call(join_kernel, [((64, PLANE), BF)], x_near, x_other)
    x_prev = lax.ppermute(x_here, "space", UP)
    x_next = lax.ppermute(x_here, "space", DOWN)

    xs, keep, send = call(
        kernel_grad_kernel,
        [((2, TAPS + 16, PLANE), BF)] + [((HALF, 128), F32)] * 2,
        x_prev,
        x_here,
        x_next,
        *cots,
        scratch=[pltpu.VMEM((384, PLANE), BF)],
    )
    r_core = lax.ppermute(send, "space", CORE)
    outs = call(forward_kernel, [((32, PLANE), F32)] * 4, xs, w_mine, w_other)
    (c_here,) = call(join_kernel, [((128, PLANE), BF)], *cots)

    half = HALF // 2
    r_send, r_keep = call(split_xlo_kernel, [((half, 128), F32)] * 2, keep, r_core)
    r_xlo = lax.ppermute(r_send, "space", XLO)
    c_prev = lax.ppermute(c_here, "space", UP)
    c_next = lax.ppermute(c_here, "space", DOWN)

    parts = call(split_y_kernel, [((PIECE, 128), F32)] * 4, r_keep, r_xlo)
    got = [lax.ppermute(parts[r], "space", along_y(r)) for r in (1, 3, 2)]
    (piece,) = call(add4_kernel, [((PIECE, 128), F32)], parts[0], *got)

    (wide_bias,) = call(bias_kernel, [((OWN, 1), F32)], bias.reshape(1, OWN))
    sums = [lax.ppermute(outs[r], "filt", along_z(r)) for r in (1, 3, 2)]
    (output,) = call(output_kernel, [((OWN, PLANE), F32)], outs[0], *sums, wide_bias)

    first = lax.ppermute(piece, ("filt", "space"), swapped(0))
    second = lax.ppermute(piece, ("filt", "space"), swapped(8))
    g_mine, g_theirs = call(
        input_grad_kernel,
        [((OWN, PLANE), F32)] * 2,
        c_prev,
        c_next,
        *cots,
        w_mine,
        w_other,
        scratch=[pltpu.VMEM((9 * 128, PLANE), BF)],
    )
    g_other = lax.ppermute(g_theirs, "filt", ACROSS)
    (grad_inputs,) = call(add2_kernel, [((OWN, PLANE), F32)], g_mine, g_other)

    (pair,) = call(pair_kernel, [((2 * PIECE, 128), F32)], piece, first, second)
    turned = {r: lax.ppermute(pair, "space", along_y(-r)) for r in (1, 3, 2)}
    (mine,) = call(join_kernel, [((HALF, 128), F32)], pair, turned[1], turned[2], turned[3])
    other = lax.ppermute(mine, "space", CORE)
    factor = float((16 * PLANE) ** -0.5)
    grad_weight, grad_bias = call(
        lambda *refs: assemble_kernel(*refs, factor=factor),
        [((864, 256), F32), ((1, OWN), F32)],
        mine,
        other,
        scratch=[pltpu.VMEM((HALF, 256), F32)],
    )
    return (
        output[None],
        grad_inputs[None],
        grad_weight.reshape(3, 3, 3, OWN, 256),
        grad_bias.reshape(OWN),
    )


def solution(mesh):
    placed = (
        P("space", "filt", None),
        P(None, None, None, "filt", None),
        P("filt"),
        P("space", "filt", None),
    )
    return jax.shard_map(
        step,
        mesh=mesh,
        in_specs=placed,
        out_specs=(
            P("space", "filt", None),
            P("space", "filt", None),
            P(None, None, None, "filt", None),
            P("filt"),
        ),
        check_vma=False,
    )
```

```python
import functools

import jax
import jax.numpy as jnp
from jax import lax
from jax.experimental import pallas as pl
from jax.experimental.pallas import tpu as pltpu
from jax.sharding import PartitionSpec as P


ROWS = 32
WIDE = 64
PLANE = ROWS * WIDE
OWN = 32
TAPS = 9 * OWN
HALF = 3 * TAPS
PIECE = HALF // 2
CODED = PIECE + 16
POWER = 12.0
TOP = 120.0
BF = jnp.bfloat16
F32 = jnp.float32

VM = pl.BlockSpec(memory_space=pltpu.VMEM)
PARAMS = pltpu.CompilerParams(vmem_limit_bytes=48 * 1024 * 1024)


def along_z(step):
    return [(f, ((f // 2 + step) % 4) * 2 + f % 2) for f in range(8)]


ACROSS = [(f, f ^ 1) for f in range(8)]
UP = [(s, (s + 1) % 16) for s in range(16)]
DOWN = [((s + 1) % 16, s) for s in range(16)]
CORE = [(s, s ^ 1) for s in range(16)]
XLO = [(s, s ^ 8) for s in range(16)]


def along_y(step):
    return [(s, (s & 9) | ((((s >> 1) + step) & 3) << 1)) for s in range(16)]


def swapped(flip):
    pairs = []
    for f in range(8):
        for s in range(16):
            if s & 1:
                pairs.append((f * 16 + s, (f ^ 1) * 16 + (s ^ flip)))
            else:
                pairs.append((f * 16 + s, f * 16 + (s ^ 8)))
    return pairs


def columns(shape):
    return lax.broadcasted_iota(jnp.int32, shape, 1) & (WIDE - 1)


def lanes(shape):
    return lax.broadcasted_iota(jnp.int32, shape, 1)


def select_kernel(w_hbm, x_hbm, c_hbm, mine_ref, theirs_ref, x_out, c_out, w_ref, sems):
    copies = [
        pltpu.make_async_copy(a, b, sems.at[i])
        for i, (a, b) in enumerate(((w_hbm, w_ref), (x_hbm, x_out), (c_hbm, c_out)))
    ]
    for copy in copies:
        copy.start()
    filt = lax.axis_index("filt")
    z, xh = filt // 2, filt % 2
    src = lax.broadcasted_iota(jnp.int32, (256, 256), 0)
    lane = lax.broadcasted_iota(jnp.int32, (256, 256), 1)
    side, turn, chan = lane >> 7, (lane >> 5) & 3, lane & 31
    want = ((z + turn) & 3) * 64 + ((xh + side) & 1) * 32 + chan
    pick = jnp.where(src == want, 1.0, 0.0).astype(BF)
    for copy in copies:
        copy.wait()
    got = jnp.dot(w_ref[...], pick, preferred_element_type=F32).astype(BF)
    mine_ref[...] = got[:, :128]
    theirs_ref[...] = got[:, 128:]


def join_kernel(*refs):
    *parts, out_ref = refs
    at = 0
    for ref in parts:
        out_ref[at : at + ref.shape[0], :] = ref[...]
        at += ref.shape[0]


def forward_kernel(xs_ref, wa_ref, wb_ref, o0, o1, o2, o3):
    rhs = jnp.concatenate([xs_ref[0, :TAPS, :], xs_ref[1, :TAPS, :]], axis=0)
    parts = []
    for kh in range(3):
        lhs = jnp.concatenate(
            [w[(kd * 3 + kh) * 96 : (kd * 3 + kh) * 96 + 96, :] for w in (wa_ref, wb_ref) for kd in range(3)],
            axis=0,
        )
        parts.append(
            lax.dot_general(lhs, rhs, (((0,), (0,)), ((), ())), preferred_element_type=F32)
        )
    lane = lanes((128, PLANE))
    total = (
        parts[1]
        + jnp.where(lane < WIDE, 0.0, pltpu.roll(parts[0], WIDE, 1))
        + jnp.where(lane >= PLANE - WIDE, 0.0, pltpu.roll(parts[2], PLANE - WIDE, 1))
    )
    for r, ref in enumerate((o0, o1, o2, o3)):
        ref[...] = total[r * 32 : r * 32 + 32]


def row_shifts(wide):
    lane = lanes(wide.shape)
    turned = pltpu.roll(wide, PLANE - WIDE, 1)
    up = jnp.where(lane >= PLANE - WIDE, 0.0, turned)
    down = jnp.where(lane < WIDE, 0.0, pltpu.roll(wide, WIDE, 1))
    return up.astype(BF), wide.astype(BF), down.astype(BF)


def kernel_grad_kernel(prev_ref, here_ref, next_ref, c0, c1, c2, c3, xs_ref, keep_ref, send_ref, cs_ref):
    space = lax.axis_index("space")
    core = space & 1
    col = columns((64, PLANE))
    has_prev = (space > 0).astype(F32)
    has_next = (space < 15).astype(F32)
    for kd, ref in enumerate((prev_ref, here_ref, next_ref)):
        wide = ref[...].astype(F32)
        if kd == 0:
            wide = wide * has_prev
        if kd == 2:
            wide = wide * has_next
        left = jnp.where(col == 0, 0.0, pltpu.roll(wide, 1, 1))
        right = jnp.where(col == WIDE - 1, 0.0, pltpu.roll(wide, PLANE - 1, 1))
        for kw, part in enumerate((left, wide, right)):
            at = (kd * 3 + kw) * OWN
            narrow = part.astype(BF)
            xs_ref[0, at : at + OWN, :] = narrow[:OWN]
            xs_ref[1, at : at + OWN, :] = narrow[OWN:]
    xs_ref[:, TAPS:, :] = jnp.ones((2, 16, PLANE), BF)
    for r, ref in enumerate((c0, c1, c2, c3)):
        for kh, part in enumerate(row_shifts(ref[...].astype(F32))):
            cs_ref[kh * 128 + r * 32 : kh * 128 + r * 32 + 32, :] = part
    for slot, ref in enumerate((keep_ref, send_ref)):
        got = lax.dot_general(
            xs_ref[core ^ slot], cs_ref[...], (((1,), (1,)), ((), ())), preferred_element_type=F32
        )
        for kh in range(3):
            ref[kh * TAPS : (kh + 1) * TAPS, :] = got[:TAPS, kh * 128 : kh * 128 + 128]
        ref[HALF:, :] = got[TAPS : TAPS + 8, 128:256]


def input_grad_kernel(prev_ref, next_ref, c0, c1, c2, c3, wa_ref, wb_ref, mine_ref, theirs_ref, cs_ref):
    space = lax.axis_index("space")
    has_prev = (space > 0).astype(F32)
    has_next = (space < 15).astype(F32)
    for r, ref in enumerate((c0, c1, c2, c3)):
        rows = slice(r * 32, r * 32 + 32)
        planes = (
            next_ref[rows, :].astype(F32) * has_next,
            ref[...].astype(F32),
            prev_ref[rows, :].astype(F32) * has_prev,
        )
        for kd, wide in enumerate(planes):
            for kh, part in enumerate(row_shifts(wide)):
                at = (kd * 3 + kh) * 128 + r * 32
                cs_ref[at : at + 32, :] = part
    lhs = jnp.concatenate(
        [
            jnp.concatenate([w[t * 96 : t * 96 + 96, :] for t in range(9)], axis=1)
            for w in (wa_ref, wb_ref)
        ],
        axis=0,
    )
    got = jnp.dot(lhs, cs_ref[...], preferred_element_type=F32)
    col = columns((OWN, PLANE))
    for h, ref in enumerate((mine_ref, theirs_ref)):
        base = h * 96
        ref[...] = (
            got[base + 32 : base + 64]
            + jnp.where(col == WIDE - 1, 0.0, pltpu.roll(got[base : base + 32], PLANE - 1, 1))
            + jnp.where(col == 0, 0.0, pltpu.roll(got[base + 64 : base + 96], 1, 1))
        )


def encode(wide):
    size = jnp.abs(wide)
    scale = jnp.max(jnp.max(size, axis=1, keepdims=True), axis=0, keepdims=True)
    scale = jnp.maximum(scale, 1e-30).astype(BF).astype(F32)
    coded = jnp.exp2(jnp.log2(size * (1.0 / scale)) * POWER + TOP)
    return jnp.where(wide < 0, -coded, coded).astype(BF), scale


def decode(coded, scale):
    wide = coded.astype(F32)
    size = scale * jnp.exp2((jnp.log2(jnp.abs(wide)) - TOP) * (1.0 / POWER))
    return jnp.where(wide < 0, -size, size)


def write_coded(out_ref, wide, bias):
    coded, scale = encode(wide)
    high = bias.astype(BF).astype(F32)
    low = bias - high
    row = lax.broadcasted_iota(jnp.int32, (16, 128), 0)
    tail = jnp.where(row == 0, scale, jnp.where(row == 1, high, jnp.where(row == 2, low, 0.0)))
    out_ref[:PIECE, :] = coded
    out_ref[PIECE:, :] = tail.astype(BF)


def read_coded(ref, at=0):
    tail = ref[at + PIECE : at + CODED, :].astype(F32)
    return decode(ref[at : at + PIECE, :], tail[0:1, 0:1]), tail[1:2, :] + tail[2:3, :]


def split_xlo_kernel(keep_ref, got_ref, send_out, keep_out):
    xlo = lax.axis_index("space") // 8
    bias = keep_ref[HALF:, :] + got_ref[HALF:, :]
    for out, at in ((send_out, (1 - xlo) * PIECE), (keep_out, xlo * PIECE)):
        rows = pl.ds(pl.multiple_of(at, 8), PIECE)
        out[:PIECE, :] = keep_ref[rows, :] + got_ref[rows, :]
        out[PIECE:, :] = bias


def code_kernel(keep_ref, got_ref, out_ref):
    write_coded(
        out_ref,
        keep_ref[:PIECE, :] + got_ref[:PIECE, :],
        keep_ref[PIECE : PIECE + 1, :] + got_ref[PIECE : PIECE + 1, :],
    )


def piece_kernel(own_ref, y1_ref, y2_ref, y3_ref, out_ref, bias_ref, *, factor):
    own, y1, y2, y3 = (read_coded(r) for r in (own_ref, y1_ref, y2_ref, y3_ref))
    wide, bias = ((own[i] + y2[i]) + (y1[i] + y3[i]) for i in range(2))
    write_coded(out_ref, wide * factor, bias)
    bias_ref[...] = bias[:, :OWN] * factor


def pair_kernel(piece_ref, first_ref, second_ref, out_ref):
    even = (lax.axis_index("space") & 1) == 0
    out_ref[:CODED, :] = jnp.where(even, piece_ref[...], first_ref[...])
    out_ref[CODED:, :] = jnp.where(even, first_ref[...], second_ref[...])


def place(pair_ref, out_ref, lane):
    xlo = lax.axis_index("space") // 8
    for rx in range(2):
        to = pl.multiple_of((xlo ^ rx) * PIECE, 8)
        out_ref[pl.ds(to, PIECE), lane : lane + 128] = read_coded(pair_ref, rx * CODED)[0]


def decode_kernel(pair_ref, out_ref):
    place(pair_ref, out_ref, 0)


def assemble_kernel(own_ref, other_ref, grad_ref, both_ref):
    filt, space = lax.axis_index("filt"), lax.axis_index("space")
    z, xh, core = filt // 2, filt % 2, space & 1
    both_ref[:, :128] = own_ref[...]
    place(other_ref, both_ref, 128)
    src = lax.broadcasted_iota(jnp.int32, (256, 256), 0)
    lane = lax.broadcasted_iota(jnp.int32, (256, 256), 1)
    side, turn, chan = src >> 7, (src >> 5) & 3, src & 31
    want = ((z + turn) & 3) * 64 + ((xh + core + side) & 1) * 32 + chan
    pick = jnp.where(lane == want, 1.0, 0.0).astype(BF)
    left = both_ref[...]
    got = jnp.zeros(left.shape, F32)
    for _ in range(3):
        part = left.astype(BF)
        left = left - part.astype(F32)
        got = got + jnp.dot(part, pick, preferred_element_type=F32)
    for kd in range(3):
        for kh in range(3):
            grad_ref[(kd * 3 + kh) * 96 : (kd * 3 + kh) * 96 + 96, :] = got[
                kh * TAPS + kd * 96 : kh * TAPS + kd * 96 + 96
            ]


def bias_kernel(ref, out):
    row = lax.broadcasted_iota(jnp.int32, (OWN, OWN), 0)
    col = lax.broadcasted_iota(jnp.int32, (OWN, OWN), 1)
    wide = jnp.where(row == col, ref[...].astype(F32), 0.0)
    out[...] = jnp.sum(wide, axis=1, keepdims=True)


def output_kernel(a, b, c, d, bias_ref, out):
    out[...] = (a[...] + b[...]) + (c[...] + d[...]) + bias_ref[...]


def add2_kernel(a, b, out):
    out[...] = a[...] + b[...]


def call(kernel, outs, *args, scratch=(), space=VM):
    return pl.pallas_call(
        kernel,
        out_shape=[jax.ShapeDtypeStruct(s, d) for s, d in outs],
        in_specs=[space] * len(args),
        out_specs=[VM] * len(outs),
        scratch_shapes=list(scratch),
        compiler_params=PARAMS,
    )(*args)


def step(inputs, weight, bias, cotangent):
    x_own = inputs[0]
    c_own = cotangent[0]

    x_other = lax.ppermute(x_own, "filt", ACROSS)
    c1, c3, c2 = (lax.ppermute(c_own, "filt", along_z(-r)) for r in (1, 3, 2))
    w_mine, w_theirs, x_near, c_near = call(
        select_kernel,
        [((864, 128), BF), ((864, 128), BF), ((OWN, PLANE), BF), ((OWN, PLANE), BF)],
        *(pltpu.with_memory_space_constraint(v, pltpu.HBM) for v in (weight.reshape(864, 256), x_own, c_own)),
        scratch=[pltpu.VMEM((864, 256), BF), pltpu.SemaphoreType.DMA((3,))],
        space=pl.BlockSpec(memory_space=pltpu.HBM),
    )
    w_other = lax.ppermute(w_theirs, "filt", ACROSS)
    cots = [c_near, c1, c2, c3]

    (x_here,) = call(join_kernel, [((64, PLANE), BF)], x_near, x_other)
    x_prev = lax.ppermute(x_here, "space", UP)
    x_next = lax.ppermute(x_here, "space", DOWN)

    xs, keep, send = call(
        kernel_grad_kernel,
        [((2, TAPS + 16, PLANE), BF)] + [((HALF + 8, 128), F32)] * 2,
        x_prev,
        x_here,
        x_next,
        *cots,
        scratch=[pltpu.VMEM((384, PLANE), BF)],
    )
    r_core = lax.ppermute(send, "space", CORE)
    outs = call(forward_kernel, [((32, PLANE), F32)] * 4, xs, w_mine, w_other)
    (c_here,) = call(join_kernel, [((128, PLANE), BF)], *cots)

    r_send, r_keep = call(split_xlo_kernel, [((PIECE + 8, 128), F32)] * 2, keep, r_core)
    r_xlo = lax.ppermute(r_send, "space", XLO)
    c_prev = lax.ppermute(c_here, "space", UP)
    c_next = lax.ppermute(c_here, "space", DOWN)

    (mine_y,) = call(code_kernel, [((CODED, 128), BF)], r_keep, r_xlo)
    y1, y3, y2 = (lax.ppermute(mine_y, "space", along_y(-r)) for r in (1, 3, 2))
    factor = float((16 * PLANE) ** -0.5)
    piece, grad_bias = call(
        functools.partial(piece_kernel, factor=factor),
        [((CODED, 128), BF), ((1, OWN), F32)],
        mine_y,
        y1,
        y2,
        y3,
    )

    (wide_bias,) = call(bias_kernel, [((OWN, 1), F32)], bias.reshape(1, OWN))
    sums = [lax.ppermute(outs[r], "filt", along_z(r)) for r in (1, 3, 2)]
    (output,) = call(output_kernel, [((OWN, PLANE), F32)], outs[0], *sums, wide_bias)

    first = lax.ppermute(piece, ("filt", "space"), swapped(0))
    second = lax.ppermute(piece, ("filt", "space"), swapped(8))
    g_mine, g_theirs = call(
        input_grad_kernel,
        [((OWN, PLANE), F32)] * 2,
        c_prev,
        c_next,
        *cots,
        w_mine,
        w_other,
        scratch=[pltpu.VMEM((9 * 128, PLANE), BF)],
    )
    g_other = lax.ppermute(g_theirs, "filt", ACROSS)
    (grad_inputs,) = call(add2_kernel, [((OWN, PLANE), F32)], g_mine, g_other)

    (pair,) = call(pair_kernel, [((2 * CODED, 128), BF)], piece, first, second)
    other = lax.ppermute(pair, "space", CORE)
    (mine,) = call(decode_kernel, [((HALF, 128), F32)], pair)
    (grad_weight,) = call(
        assemble_kernel, [((HALF, 256), F32)], mine, other, scratch=[pltpu.VMEM((HALF, 256), F32)]
    )
    return (
        output[None],
        grad_inputs[None],
        grad_weight.reshape(3, 3, 3, OWN, 256),
        grad_bias.reshape(OWN),
    )


def solution(mesh):
    placed = (
        P("space", "filt", None),
        P(None, None, None, "filt", None),
        P("filt"),
        P("space", "filt", None),
    )
    return jax.shard_map(
        step,
        mesh=mesh,
        in_specs=placed,
        out_specs=(
            P("space", "filt", None),
            P("space", "filt", None),
            P(None, None, None, "filt", None),
            P("filt"),
        ),
        check_vma=False,
    )
```

```python
import functools

import jax
import jax.numpy as jnp
from jax import lax
from jax.experimental import pallas as pl
from jax.experimental.pallas import tpu as pltpu
from jax.sharding import PartitionSpec as P


ROWS = 32
WIDE = 64
PLANE = ROWS * WIDE
OWN = 32
TAPS = 9 * OWN
HALF = 3 * TAPS
PIECE = HALF // 2
CODED = PIECE + 16
POWER = 15.0
TOP = 120.0
BF = jnp.bfloat16
F32 = jnp.float32

VM = pl.BlockSpec(memory_space=pltpu.VMEM)
PARAMS = pltpu.CompilerParams(vmem_limit_bytes=48 * 1024 * 1024)


def along_z(step):
    return [(f, ((f // 2 + step) % 4) * 2 + f % 2) for f in range(8)]


ACROSS = [(f, f ^ 1) for f in range(8)]
BESIDE = [(s, (s + 1) % 16 if s & 1 else (s - 1) % 16) for s in range(16)]
CORE = [(s, s ^ 1) for s in range(16)]
XLO = [(s, s ^ 8) for s in range(16)]


def along_y(step):
    return [(s, (s & 9) | ((((s >> 1) + step) & 3) << 1)) for s in range(16)]


def crossing(flip, idle):
    return [
        (f * 16 + s, (f ^ 1) * 16 + (s ^ flip) if s & 1 else f * 16 + (s ^ idle))
        for f in range(8)
        for s in range(16)
    ]


def columns(shape):
    return lax.broadcasted_iota(jnp.int32, shape, 1) & (WIDE - 1)


def lanes(shape):
    return lax.broadcasted_iota(jnp.int32, shape, 1)


def select_kernel(w_hbm, x_hbm, c_hbm, mine_ref, theirs_ref, x_out, c_out, w_ref, sems):
    copies = [
        pltpu.make_async_copy(a, b, sems.at[i])
        for i, (a, b) in enumerate(((w_hbm, w_ref), (x_hbm, x_out), (c_hbm, c_out)))
    ]
    for copy in copies:
        copy.start()
    filt = lax.axis_index("filt")
    z, xh = filt // 2, filt % 2
    src = lax.broadcasted_iota(jnp.int32, (256, 256), 0)
    lane = lax.broadcasted_iota(jnp.int32, (256, 256), 1)
    side, turn, chan = lane >> 7, (lane >> 5) & 3, lane & 31
    want = ((z + turn) & 3) * 64 + ((xh + side) & 1) * 32 + chan
    pick = jnp.where(src == want, 1.0, 0.0).astype(BF)
    for copy in copies:
        copy.wait()
    got = jnp.dot(w_ref[...], pick, preferred_element_type=F32).astype(BF)
    mine_ref[...] = got[:, :128]
    theirs_ref[...] = got[:, 128:]


def join_kernel(*refs):
    *parts, out_ref = refs
    at = 0
    for ref in parts:
        out_ref[at : at + ref.shape[0], :] = ref[...]
        at += ref.shape[0]


def forward_kernel(xs_ref, wa_ref, wb_ref, o0, o1, o2, o3):
    rhs = jnp.concatenate([xs_ref[0, :TAPS, :], xs_ref[1, :TAPS, :]], axis=0)
    parts = []
    for kh in range(3):
        lhs = jnp.concatenate(
            [w[(kd * 3 + kh) * 96 : (kd * 3 + kh) * 96 + 96, :] for w in (wa_ref, wb_ref) for kd in range(3)],
            axis=0,
        )
        parts.append(
            lax.dot_general(lhs, rhs, (((0,), (0,)), ((), ())), preferred_element_type=F32)
        )
    lane = lanes((128, PLANE))
    total = (
        parts[1]
        + jnp.where(lane < WIDE, 0.0, pltpu.roll(parts[0], WIDE, 1))
        + jnp.where(lane >= PLANE - WIDE, 0.0, pltpu.roll(parts[2], PLANE - WIDE, 1))
    )
    for r, ref in enumerate((o0, o1, o2, o3)):
        ref[...] = total[r * 32 : r * 32 + 32]


def row_shifts(wide):
    lane = lanes(wide.shape)
    turned = pltpu.roll(wide, PLANE - WIDE, 1)
    up = jnp.where(lane >= PLANE - WIDE, 0.0, turned)
    down = jnp.where(lane < WIDE, 0.0, pltpu.roll(wide, WIDE, 1))
    return up.astype(BF), wide.astype(BF), down.astype(BF)


def beside():
    space = lax.axis_index("space")
    inside = jnp.logical_and(space != 0, space != 15).astype(F32)
    return inside, (space & 1) == 0


def kernel_grad_kernel(chip_ref, here_ref, far_ref, c0, c1, c2, c3, xs_ref, keep_ref, send_ref, cs_ref):
    core = lax.axis_index("space") & 1
    col = columns((64, PLANE))
    inside, even = beside()
    for ref, kd in ((chip_ref, jnp.where(even, 2, 0)), (here_ref, 1), (far_ref, jnp.where(even, 0, 2))):
        wide = ref[...].astype(F32)
        if ref is far_ref:
            wide = wide * inside
        left = jnp.where(col == 0, 0.0, pltpu.roll(wide, 1, 1))
        right = jnp.where(col == WIDE - 1, 0.0, pltpu.roll(wide, PLANE - 1, 1))
        for kw, part in enumerate((left, wide, right)):
            rows = pl.ds(pl.multiple_of((kd * 3 + kw) * OWN, OWN), OWN)
            narrow = part.astype(BF)
            xs_ref[0, rows, :] = narrow[:OWN]
            xs_ref[1, rows, :] = narrow[OWN:]
    xs_ref[:, TAPS:, :] = jnp.ones((2, 16, PLANE), BF)
    for r, ref in enumerate((c0, c1, c2, c3)):
        for kh, part in enumerate(row_shifts(ref[...].astype(F32))):
            cs_ref[kh * 128 + r * 32 : kh * 128 + r * 32 + 32, :] = part
    for slot, ref in enumerate((keep_ref, send_ref)):
        got = lax.dot_general(
            xs_ref[core ^ slot], cs_ref[...], (((1,), (1,)), ((), ())), preferred_element_type=F32
        )
        for kh in range(3):
            ref[kh * TAPS : (kh + 1) * TAPS, :] = got[:TAPS, kh * 128 : kh * 128 + 128]
        ref[HALF:, :] = got[TAPS : TAPS + 8, 128:256]


def input_grad_kernel(chip_ref, far_ref, c0, c1, c2, c3, wa_ref, wb_ref, mine_ref, theirs_ref, cs_ref):
    inside, even = beside()
    for r, ref in enumerate((c0, c1, c2, c3)):
        rows = slice(r * 32, r * 32 + 32)
        planes = (
            chip_ref[rows, :].astype(F32),
            ref[...].astype(F32),
            far_ref[rows, :].astype(F32) * inside,
        )
        for kd, wide in enumerate(planes):
            for kh, part in enumerate(row_shifts(wide)):
                at = (kd * 3 + kh) * 128 + r * 32
                cs_ref[at : at + 32, :] = part

    def taps(w, kd, kh):
        ahead, here, behind = (w[(k * 3 + kh) * 96 : (k * 3 + kh) * 96 + 96, :] for k in range(3))
        if kd == 1:
            return here
        first, second = (ahead, behind) if kd == 0 else (behind, ahead)
        return jnp.where(even, first, second)

    lhs = jnp.concatenate(
        [
            jnp.concatenate([taps(w, kd, kh) for kd in range(3) for kh in range(3)], axis=1)
            for w in (wa_ref, wb_ref)
        ],
        axis=0,
    )
    got = jnp.dot(lhs, cs_ref[...], preferred_element_type=F32)
    col = columns((OWN, PLANE))
    for h in range(2):
        base = h * 96
        part = (
            got[base + 32 : base + 64]
            + jnp.where(col == WIDE - 1, 0.0, pltpu.roll(got[base : base + 32], PLANE - 1, 1))
            + jnp.where(col == 0, 0.0, pltpu.roll(got[base + 64 : base + 96], 1, 1))
        )
        if h == 0:
            mine_ref[...] = part
        else:
            theirs_ref[:, :PLANE], scale = encode(part)
            theirs_ref[:, PLANE:] = jnp.broadcast_to(scale, (OWN, 128)).astype(BF)


def encode(wide):
    size = jnp.abs(wide)
    scale = jnp.max(jnp.max(size, axis=1, keepdims=True), axis=0, keepdims=True)
    scale = jnp.maximum(scale, 1e-30).astype(BF).astype(F32)
    coded = jnp.exp2(jnp.log2(size * (1.0 / scale)) * POWER + TOP)
    return jnp.where(wide < 0, -coded, coded).astype(BF), scale


def decode(coded, scale):
    wide = coded.astype(F32)
    size = scale * jnp.exp2((jnp.log2(jnp.abs(wide)) - TOP) * (1.0 / POWER))
    return jnp.where(wide < 0, -size, size)


def write_coded(out_ref, wide, bias):
    coded, scale = encode(wide)
    high = bias.astype(BF).astype(F32)
    low = bias - high
    row = lax.broadcasted_iota(jnp.int32, (16, 128), 0)
    tail = jnp.where(row == 0, scale, jnp.where(row == 1, high, jnp.where(row == 2, low, 0.0)))
    out_ref[:PIECE, :] = coded
    out_ref[PIECE:, :] = tail.astype(BF)


def read_coded(ref, at=0):
    tail = ref[at + PIECE : at + CODED, :].astype(F32)
    return decode(ref[at : at + PIECE, :], tail[0:1, 0:1]), tail[1:2, :] + tail[2:3, :]


def split_xlo_kernel(keep_ref, got_ref, send_out, cross_out, keep_out):
    xlo = lax.axis_index("space") // 8
    bias = keep_ref[HALF:, :] + got_ref[HALF:, :]
    send, keep = (
        keep_ref[rows, :] + got_ref[rows, :]
        for rows in (pl.ds(pl.multiple_of(at, 8), PIECE) for at in ((1 - xlo) * PIECE, xlo * PIECE))
    )
    write_coded(send_out, send, bias[:1])
    write_coded(cross_out, keep, bias[:1])
    keep_out[:PIECE, :] = keep
    keep_out[PIECE:, :] = bias


def code_kernel(keep_ref, near_ref, far_ref, out_ref):
    even = (lax.axis_index("space") & 1) == 0
    near, far = read_coded(near_ref), read_coded(far_ref)
    write_coded(
        out_ref,
        jnp.where(even, keep_ref[:PIECE, :], near[0]) + far[0],
        jnp.where(even, keep_ref[PIECE : PIECE + 1, :], near[1]) + far[1],
    )


def piece_kernel(own_ref, y1_ref, y2_ref, y3_ref, out_ref, *, factor):
    own, y1, y2, y3 = (read_coded(r) for r in (own_ref, y1_ref, y2_ref, y3_ref))
    wide, bias = ((own[i] + y2[i]) + (y1[i] + y3[i]) for i in range(2))
    z = lax.axis_index("filt") // 2
    write_coded(out_ref, pltpu.roll(wide * factor, z * 32, 1), bias * factor)


def place(pair_ref, out_ref):
    xlo = lax.axis_index("space") // 8
    for rx in range(2):
        to = pl.multiple_of((xlo ^ rx) * PIECE, 8)
        wide, bias = read_coded(pair_ref, rx * CODED)
        out_ref[pl.ds(to, PIECE), :] = wide
    return bias[:, :OWN]


def side_of(swap):
    return (lax.axis_index("filt") ^ lax.axis_index("space") ^ swap) & 1


def spread(wide, side):
    first, second, third, fourth = (
        pltpu.roll(wide, ((side + j) & 3) * 32, 1) for j in range(4)
    )
    low = lanes(wide.shape) < 64
    return jnp.where(low, first, second), jnp.where(low, third, fourth)


def decode_kernel(pair_ref, out_ref, bias_ref, half_ref):
    bias_ref[...] = place(pair_ref, half_ref)
    out_ref[:, :128], out_ref[:, 128:] = spread(half_ref[...], side_of(0))


def assemble_kernel(own_ref, own_bias_ref, other_ref, grad_hbm, bias_ref, half_ref, grad_ref, sems):
    bias = place(other_ref, half_ref)
    core = lax.axis_index("space") & 1
    bias_ref[...] = jnp.where(core == 0, own_bias_ref[...], bias)
    side = side_of(1)
    theirs = ((lanes((TAPS, 128)) >> 5) & 1) == side
    copies = []
    for kh in range(3):
        rows = slice(kh * TAPS, kh * TAPS + TAPS)
        for t, part in enumerate(spread(half_ref[rows, :], side)):
            cols = slice(t * 128, t * 128 + 128)
            whole = jnp.where(theirs, part, own_ref[rows, cols])
            grad_ref[kh, :, :, cols] = whole.reshape(3, 96, 128)
        copies.append(pltpu.make_async_copy(grad_ref.at[kh], grad_hbm.at[:, kh], sems.at[kh]))
        copies[-1].start()
    for copy in copies:
        copy.wait()


def bias_kernel(ref, out):
    row = lax.broadcasted_iota(jnp.int32, (OWN, OWN), 0)
    col = lax.broadcasted_iota(jnp.int32, (OWN, OWN), 1)
    wide = jnp.where(row == col, ref[...].astype(F32), 0.0)
    out[...] = jnp.sum(wide, axis=1, keepdims=True)


def biased_kernel(ref, bias_ref, out):
    out[...] = ref[...] + bias_ref[...]


def sums_kernel(a, b, c, d, mine_ref, theirs_ref, out, grad):
    out[...] = (a[...] + b[...]) + (c[...] + d[...])
    scale = theirs_ref[0:1, PLANE : PLANE + 1].astype(F32)
    grad[...] = mine_ref[...] + decode(theirs_ref[:, :PLANE], scale)


def call(kernel, outs, *args, scratch=(), space=VM, out_space=VM):
    return pl.pallas_call(
        kernel,
        out_shape=[jax.ShapeDtypeStruct(s, d) for s, d in outs],
        in_specs=[space] * len(args),
        out_specs=[out_space] + [VM] * (len(outs) - 1),
        scratch_shapes=list(scratch),
        compiler_params=PARAMS,
    )(*args)


def step(inputs, weight, bias, cotangent):
    x_own = inputs[0]
    c_own = cotangent[0]

    x_other = lax.ppermute(x_own, "filt", ACROSS)
    c1, c3, c2 = (lax.ppermute(c_own, "filt", along_z(-r)) for r in (1, 3, 2))
    w_mine, w_theirs, x_near, c_near = call(
        select_kernel,
        [((864, 128), BF), ((864, 128), BF), ((OWN, PLANE), BF), ((OWN, PLANE), BF)],
        *(pltpu.with_memory_space_constraint(v, pltpu.HBM) for v in (weight.reshape(864, 256), x_own, c_own)),
        scratch=[pltpu.VMEM((864, 256), BF), pltpu.SemaphoreType.DMA((3,))],
        space=pl.BlockSpec(memory_space=pltpu.HBM),
    )
    w_other = lax.ppermute(w_theirs, "filt", ACROSS)
    cots = [c_near, c1, c2, c3]

    (x_here,) = call(join_kernel, [((64, PLANE), BF)], x_near, x_other)
    x_chip = lax.ppermute(x_here, "space", CORE)
    x_far = lax.ppermute(x_here, "space", BESIDE)

    xs, keep, send = call(
        kernel_grad_kernel,
        [((2, TAPS + 16, PLANE), BF)] + [((HALF + 8, 128), F32)] * 2,
        x_chip,
        x_here,
        x_far,
        *cots,
        scratch=[pltpu.VMEM((384, PLANE), BF)],
    )
    r_core = lax.ppermute(send, "space", CORE)
    outs = call(forward_kernel, [((32, PLANE), F32)] * 4, xs, w_mine, w_other)
    (c_here,) = call(join_kernel, [((128, PLANE), BF)], *cots)

    r_send, r_cross, r_keep = call(
        split_xlo_kernel, [((CODED, 128), BF)] * 2 + [((PIECE + 8, 128), F32)], keep, r_core
    )
    r_far = lax.ppermute(r_send, ("filt", "space"), crossing(8, 8))
    r_near = lax.ppermute(r_cross, ("filt", "space"), crossing(0, 2))
    c_chip = lax.ppermute(c_here, "space", CORE)
    c_far = lax.ppermute(c_here, "space", BESIDE)

    (mine_y,) = call(code_kernel, [((CODED, 128), BF)], r_keep, r_near, r_far)
    y1, y3, y2 = (lax.ppermute(mine_y, "space", along_y(-r)) for r in (1, 3, 2))
    factor = float((16 * PLANE) ** -0.5)
    (piece,) = call(
        functools.partial(piece_kernel, factor=factor), [((CODED, 128), BF)], mine_y, y1, y2, y3
    )

    (wide_bias,) = call(bias_kernel, [((OWN, 1), F32)], bias.reshape(1, OWN))
    (biased,) = call(biased_kernel, [((OWN, PLANE), F32)], outs[0], wide_bias)
    sums = [lax.ppermute(outs[r], "filt", along_z(r)) for r in (1, 3, 2)]
    g_mine, g_theirs = call(
        input_grad_kernel,
        [((OWN, PLANE), F32), ((OWN, PLANE + 128), BF)],
        c_chip,
        c_far,
        *cots,
        w_mine,
        w_other,
        scratch=[pltpu.VMEM((9 * 128, PLANE), BF)],
    )
    g_other = lax.ppermute(g_theirs, "filt", ACROSS)
    output, grad_inputs = call(
        sums_kernel, [((OWN, PLANE), F32)] * 2, biased, *sums, g_mine, g_other
    )

    piece_far = lax.ppermute(piece, "space", XLO)
    (pair,) = call(join_kernel, [((2 * CODED, 128), BF)], piece, piece_far)
    other = lax.ppermute(pair, "space", CORE)
    mine, mine_bias = call(
        decode_kernel,
        [((HALF, 256), F32), ((1, OWN), F32)],
        pair,
        scratch=[pltpu.VMEM((HALF, 128), F32)],
    )
    grad_weight, grad_bias = call(
        assemble_kernel,
        [((3, 3, 96, 256), F32), ((1, OWN), F32)],
        mine,
        mine_bias,
        other,
        scratch=[
            pltpu.VMEM((HALF, 128), F32),
            pltpu.VMEM((3, 3, 96, 256), F32),
            pltpu.SemaphoreType.DMA((3,)),
        ],
        out_space=pl.BlockSpec(memory_space=pltpu.HBM),
    )
    return (
        output[None],
        grad_inputs[None],
        grad_weight.reshape(3, 3, 3, OWN, 256),
        grad_bias.reshape(OWN),
    )


def solution(mesh):
    placed = (
        P("space", "filt", None),
        P(None, None, None, "filt", None),
        P("filt"),
        P("space", "filt", None),
    )
    return jax.shard_map(
        step,
        mesh=mesh,
        in_specs=placed,
        out_specs=(
            P("space", "filt", None),
            P("space", "filt", None),
            P(None, None, None, "filt", None),
            P("filt"),
        ),
        check_vma=False,
    )
```

```python
import functools

import jax
import jax.numpy as jnp
from jax import lax
from jax.experimental import pallas as pl
from jax.experimental.pallas import tpu as pltpu
from jax.sharding import PartitionSpec as P


ROWS = 32
WIDE = 64
PLANE = ROWS * WIDE
OWN = 32
TAPS = 9 * OWN
HALF = 3 * TAPS
PIECE = HALF // 2
CODED = PIECE + 16
POWER = 15.0
TOP = 120.0
BF = jnp.bfloat16
F32 = jnp.float32

VM = pl.BlockSpec(memory_space=pltpu.VMEM)
PARAMS = pltpu.CompilerParams(vmem_limit_bytes=48 * 1024 * 1024)


def along_z(step):
    return [(f, ((f // 2 + step) % 4) * 2 + f % 2) for f in range(8)]


Z_FIRST = [(f, f ^ 2) for f in range(8)]
Z_SECOND = [(f, f ^ 6) for f in range(8)]
ACROSS = [(f, f ^ 1) for f in range(8)]
BESIDE = [(s, (s + 1) % 16 if s & 1 else (s - 1) % 16) for s in range(16)]
CORE = [(s, s ^ 1) for s in range(16)]
XLO = [(s, s ^ 8) for s in range(16)]


def along_y(step):
    return [(s, (s & 9) | ((((s >> 1) + step) & 3) << 1)) for s in range(16)]


def crossing(flip, idle):
    return [
        (f * 16 + s, (f ^ 1) * 16 + (s ^ flip) if s & 1 else f * 16 + (s ^ idle))
        for f in range(8)
        for s in range(16)
    ]


def columns(shape):
    return lax.broadcasted_iota(jnp.int32, shape, 1) & (WIDE - 1)


def lanes(shape):
    return lax.broadcasted_iota(jnp.int32, shape, 1)


def select_kernel(w_hbm, x_hbm, c_hbm, mine_ref, theirs_ref, x_out, c_out, w_ref, sems):
    copies = [
        pltpu.make_async_copy(a, b, sems.at[i])
        for i, (a, b) in enumerate(((w_hbm, w_ref), (x_hbm, x_out), (c_hbm, c_out)))
    ]
    for copy in copies:
        copy.start()
    filt = lax.axis_index("filt")
    z, xh = filt // 2, filt % 2
    src = lax.broadcasted_iota(jnp.int32, (256, 256), 0)
    lane = lax.broadcasted_iota(jnp.int32, (256, 256), 1)
    side, turn, chan = lane >> 7, (lane >> 5) & 3, lane & 31
    want = ((z + turn) & 3) * 64 + ((xh + side) & 1) * 32 + chan
    pick = jnp.where(src == want, 1.0, 0.0).astype(BF)
    for copy in copies:
        copy.wait()
    got = jnp.dot(w_ref[...], pick, preferred_element_type=F32).astype(BF)
    mine_ref[...] = got[:, :128]
    theirs_ref[...] = got[:, 128:]


def join_kernel(*refs):
    *parts, out_ref = refs
    at = 0
    for ref in parts:
        out_ref[at : at + ref.shape[0], :] = ref[...]
        at += ref.shape[0]


def forward_kernel(xs_ref, wa_ref, wb_ref, mine_ref, first_ref, send_ref):
    rhs = jnp.concatenate([xs_ref[0, :TAPS, :], xs_ref[1, :TAPS, :]], axis=0)
    parts = []
    for kh in range(3):
        lhs = jnp.concatenate(
            [w[(kd * 3 + kh) * 96 : (kd * 3 + kh) * 96 + 96, :] for w in (wa_ref, wb_ref) for kd in range(3)],
            axis=0,
        )
        parts.append(
            lax.dot_general(lhs, rhs, (((0,), (0,)), ((), ())), preferred_element_type=F32)
        )
    lane = lanes((128, PLANE))
    total = (
        parts[1]
        + jnp.where(lane < WIDE, 0.0, pltpu.roll(parts[0], WIDE, 1))
        + jnp.where(lane >= PLANE - WIDE, 0.0, pltpu.roll(parts[2], PLANE - WIDE, 1))
    )
    even = ((lax.axis_index("filt") // 2) & 1) == 0
    near, across, far = (total[r * 32 : r * 32 + 32] for r in (1, 2, 3))
    mine_ref[...] = total[:32]
    first_ref[...] = jnp.where(even, near, far)
    write_rows(send_ref, jnp.concatenate([jnp.where(even, far, near), across], axis=0))


def row_shifts(wide):
    lane = lanes(wide.shape)
    turned = pltpu.roll(wide, PLANE - WIDE, 1)
    up = jnp.where(lane >= PLANE - WIDE, 0.0, turned)
    down = jnp.where(lane < WIDE, 0.0, pltpu.roll(wide, WIDE, 1))
    return up.astype(BF), wide.astype(BF), down.astype(BF)


def beside():
    space = lax.axis_index("space")
    inside = jnp.logical_and(space != 0, space != 15).astype(F32)
    return inside, (space & 1) == 0


def kernel_grad_kernel(chip_ref, here_ref, far_ref, c0, c1, c2, c3, xs_ref, keep_ref, send_ref, cs_ref):
    core = lax.axis_index("space") & 1
    col = columns((64, PLANE))
    inside, even = beside()
    for ref, kd in ((chip_ref, jnp.where(even, 2, 0)), (here_ref, 1), (far_ref, jnp.where(even, 0, 2))):
        wide = ref[...].astype(F32)
        if ref is far_ref:
            wide = wide * inside
        left = jnp.where(col == 0, 0.0, pltpu.roll(wide, 1, 1))
        right = jnp.where(col == WIDE - 1, 0.0, pltpu.roll(wide, PLANE - 1, 1))
        for kw, part in enumerate((left, wide, right)):
            rows = pl.ds(pl.multiple_of((kd * 3 + kw) * OWN, OWN), OWN)
            narrow = part.astype(BF)
            xs_ref[0, rows, :] = narrow[:OWN]
            xs_ref[1, rows, :] = narrow[OWN:]
    xs_ref[:, TAPS:, :] = jnp.ones((2, 16, PLANE), BF)
    for r, ref in enumerate((c0, c1, c2, c3)):
        for kh, part in enumerate(row_shifts(ref[...].astype(F32))):
            cs_ref[kh * 128 + r * 32 : kh * 128 + r * 32 + 32, :] = part
    for slot, ref in enumerate((keep_ref, send_ref)):
        got = lax.dot_general(
            xs_ref[core ^ slot], cs_ref[...], (((1,), (1,)), ((), ())), preferred_element_type=F32
        )
        for kh in range(3):
            ref[kh * TAPS : (kh + 1) * TAPS, :] = got[:TAPS, kh * 128 : kh * 128 + 128]
        ref[HALF:, :] = got[TAPS : TAPS + 8, 128:256]


def input_grad_kernel(chip_ref, far_ref, c0, c1, c2, c3, wa_ref, wb_ref, mine_ref, theirs_ref, cs_ref):
    inside, even = beside()
    for r, ref in enumerate((c0, c1, c2, c3)):
        rows = slice(r * 32, r * 32 + 32)
        planes = (
            chip_ref[rows, :].astype(F32),
            ref[...].astype(F32),
            far_ref[rows, :].astype(F32) * inside,
        )
        for kd, wide in enumerate(planes):
            for kh, part in enumerate(row_shifts(wide)):
                at = (kd * 3 + kh) * 128 + r * 32
                cs_ref[at : at + 32, :] = part

    def taps(w, kd, kh):
        ahead, here, behind = (w[(k * 3 + kh) * 96 : (k * 3 + kh) * 96 + 96, :] for k in range(3))
        if kd == 1:
            return here
        first, second = (ahead, behind) if kd == 0 else (behind, ahead)
        return jnp.where(even, first, second)

    lhs = jnp.concatenate(
        [
            jnp.concatenate([taps(w, kd, kh) for kd in range(3) for kh in range(3)], axis=1)
            for w in (wa_ref, wb_ref)
        ],
        axis=0,
    )
    got = jnp.dot(lhs, cs_ref[...], preferred_element_type=F32)
    col = columns((OWN, PLANE))
    for h in range(2):
        base = h * 96
        part = (
            got[base + 32 : base + 64]
            + jnp.where(col == WIDE - 1, 0.0, pltpu.roll(got[base : base + 32], PLANE - 1, 1))
            + jnp.where(col == 0, 0.0, pltpu.roll(got[base + 64 : base + 96], 1, 1))
        )
        if h == 0:
            mine_ref[...] = part
        else:
            write_rows(theirs_ref, part)


def encode(wide):
    size = jnp.abs(wide)
    scale = jnp.max(jnp.max(size, axis=1, keepdims=True), axis=0, keepdims=True)
    scale = jnp.maximum(scale, 1e-30).astype(BF).astype(F32)
    coded = jnp.exp2(jnp.log2(size * (1.0 / scale)) * POWER + TOP)
    return jnp.where(wide < 0, -coded, coded).astype(BF), scale


def decode(coded, scale):
    wide = coded.astype(F32)
    size = scale * jnp.exp2((jnp.log2(jnp.abs(wide)) - TOP) * (1.0 / POWER))
    return jnp.where(wide < 0, -size, size)


def write_coded(out_ref, wide, bias):
    coded, scale = encode(wide)
    high = bias.astype(BF).astype(F32)
    low = bias - high
    row = lax.broadcasted_iota(jnp.int32, (16, 128), 0)
    tail = jnp.where(row == 0, scale, jnp.where(row == 1, high, jnp.where(row == 2, low, 0.0)))
    out_ref[:PIECE, :] = coded
    out_ref[PIECE:, :] = tail.astype(BF)


def read_tail(tail):
    return tail[1:2, :] + tail[2:3, :]


def read_coded(ref):
    tail = ref[PIECE:CODED, :].astype(F32)
    return decode(ref[:PIECE, :], tail[0:1, 0:1]), read_tail(tail)


def write_rows(out_ref, wide):
    out_ref[:, :PLANE], scale = encode(wide)
    out_ref[:, PLANE:] = jnp.broadcast_to(scale, (wide.shape[0], 128)).astype(BF)


def read_rows(coded):
    return decode(coded[:, :PLANE], coded[0:1, PLANE : PLANE + 1].astype(F32))


def split_xlo_kernel(keep_ref, got_ref, send_out, cross_out, keep_out):
    xlo = lax.axis_index("space") // 8
    bias = keep_ref[HALF:, :] + got_ref[HALF:, :]
    send, keep = (
        keep_ref[rows, :] + got_ref[rows, :]
        for rows in (pl.ds(pl.multiple_of(at, 8), PIECE) for at in ((1 - xlo) * PIECE, xlo * PIECE))
    )
    write_coded(send_out, send, bias[:1])
    write_coded(cross_out, keep, bias[:1])
    keep_out[:PIECE, :] = keep
    keep_out[PIECE:, :] = bias


def code_kernel(keep_ref, near_ref, far_ref, out_ref):
    even = (lax.axis_index("space") & 1) == 0
    near, far = read_coded(near_ref), read_coded(far_ref)
    write_coded(
        out_ref,
        jnp.where(even, keep_ref[:PIECE, :], near[0]) + far[0],
        jnp.where(even, keep_ref[PIECE : PIECE + 1, :], near[1]) + far[1],
    )


def piece_kernel(own_ref, y1_ref, y2_ref, y3_ref, out_ref, *, factor):
    own, y1, y2, y3 = (read_coded(r) for r in (own_ref, y1_ref, y2_ref, y3_ref))
    wide, bias = ((own[i] + y2[i]) + (y1[i] + y3[i]) for i in range(2))
    z = lax.axis_index("filt") // 2
    write_coded(out_ref, pltpu.roll(wide * factor, z * 32, 1), bias * factor)


def side_of(swap):
    return (lax.axis_index("filt") ^ lax.axis_index("space") ^ swap) & 1


def spread(wide, side):
    first, second, third, fourth = (
        pltpu.roll(wide, ((side + j) & 3) * 32, 1) for j in range(4)
    )
    low = lanes(wide.shape) < 64
    return jnp.where(low, first, second), jnp.where(low, third, fourth)


def decode_kernel(own_ref, out_ref):
    out_ref[:, :128], out_ref[:, 128:] = spread(read_coded(own_ref)[0], side_of(0))


def write_half(turn, own_ref, got_ref, grad_hbm, rows_ref, sems):
    wide, bias = read_coded(got_ref)
    side = side_of(1)
    theirs = ((lanes((PIECE, 128)) >> 5) & 1) == side
    for t, part in enumerate(spread(wide, side)):
        cols = slice(t * 128, t * 128 + 128)
        rows_ref[:, cols] = jnp.where(theirs, part, own_ref[:, cols])
    half = (lax.axis_index("space") // 8) ^ turn
    spans = []
    for j in range(4):
        block = j + 5 * half
        to = lax.rem(block, 3) * 3 + lax.div(block, 3)
        spans.append((half * 48 + j * 96, 96, to, 0))
    spans.append(((1 - half) * 384, 48, 4, half * 48))
    copies = [
        pltpu.make_async_copy(
            rows_ref.at[pl.ds(pl.multiple_of(at, 16), size), :],
            grad_hbm.at[to, pl.ds(row if isinstance(row, int) else pl.multiple_of(row, 16), size), :],
            sems.at[i],
        )
        for i, (at, size, to, row) in enumerate(spans)
    ]
    for copy in copies:
        copy.start()
    return bias[:, :OWN], copies


def first_kernel(own_ref, piece_ref, got_ref, grad_hbm, bias_hbm, rows_ref, sems, bias_ref, bias_sem):
    bias, copies = write_half(0, own_ref, got_ref, grad_hbm, rows_ref, sems)
    core = lax.axis_index("space") & 1
    own_bias = read_tail(piece_ref[PIECE:CODED, :].astype(F32))[:, :OWN]
    bias_ref[...] = jnp.where(core == 0, own_bias, bias)
    copies.append(pltpu.make_async_copy(bias_ref, bias_hbm, bias_sem))
    copies[-1].start()
    for copy in copies:
        copy.wait()


def second_kernel(own_ref, got_ref, _, grad_hbm, rows_ref, sems):
    for copy in write_half(1, own_ref, got_ref, grad_hbm, rows_ref, sems)[1]:
        copy.wait()


def bias_kernel(ref, out):
    row = lax.broadcasted_iota(jnp.int32, (OWN, OWN), 0)
    col = lax.broadcasted_iota(jnp.int32, (OWN, OWN), 1)
    wide = jnp.where(row == col, ref[...].astype(F32), 0.0)
    out[...] = jnp.sum(wide, axis=1, keepdims=True)


def halve_kernel(mine_ref, first_ref, got_ref, sum_ref, send_ref):
    got = read_rows(got_ref[...])
    sum_ref[...] = mine_ref[...] + got[:OWN]
    write_rows(send_ref, first_ref[...] + got[OWN:])


def sums_kernel(mine_ref, got_ref, bias_ref, near_ref, theirs_ref, out_hbm, grad_hbm, out_ref, grad_ref, sems):
    copies = [
        pltpu.make_async_copy(out_ref, out_hbm, sems.at[0]),
        pltpu.make_async_copy(grad_ref, grad_hbm, sems.at[1]),
    ]
    out_ref[...] = mine_ref[...] + read_rows(got_ref[...]) + bias_ref[...]
    copies[0].start()
    grad_ref[...] = near_ref[...] + read_rows(theirs_ref[...])
    copies[1].start()
    for copy in copies:
        copy.wait()


def call(kernel, outs, *args, scratch=(), space=VM, out_space=VM, over=None):
    return pl.pallas_call(
        kernel,
        out_shape=[jax.ShapeDtypeStruct(s, d) for s, d in outs],
        in_specs=[space if i != over else out_space for i in range(len(args))],
        input_output_aliases={} if over is None else {over: 0},
        out_specs=[out_space] * len(outs),
        scratch_shapes=list(scratch),
        compiler_params=PARAMS,
    )(*args)


def step(inputs, weight, bias, cotangent):
    x_own = inputs[0]
    c_own = cotangent[0]

    x_other = lax.ppermute(x_own, "filt", ACROSS)
    c1, c3, c2 = (lax.ppermute(c_own, "filt", along_z(-r)) for r in (1, 3, 2))
    w_mine, w_theirs, x_near, c_near = call(
        select_kernel,
        [((864, 128), BF), ((864, 128), BF), ((OWN, PLANE), BF), ((OWN, PLANE), BF)],
        *(pltpu.with_memory_space_constraint(v, pltpu.HBM) for v in (weight.reshape(864, 256), x_own, c_own)),
        scratch=[pltpu.VMEM((864, 256), BF), pltpu.SemaphoreType.DMA((3,))],
        space=pl.BlockSpec(memory_space=pltpu.HBM),
    )
    w_other = lax.ppermute(w_theirs, "filt", ACROSS)
    cots = [c_near, c1, c2, c3]

    (x_here,) = call(join_kernel, [((64, PLANE), BF)], x_near, x_other)
    x_chip = lax.ppermute(x_here, "space", CORE)
    x_far = lax.ppermute(x_here, "space", BESIDE)

    xs, keep, send = call(
        kernel_grad_kernel,
        [((2, TAPS + 16, PLANE), BF)] + [((HALF + 8, 128), F32)] * 2,
        x_chip,
        x_here,
        x_far,
        *cots,
        scratch=[pltpu.VMEM((384, PLANE), BF)],
    )
    r_core = lax.ppermute(send, "space", CORE)
    o_mine, o_first, o_send = call(
        forward_kernel,
        [((OWN, PLANE), F32)] * 2 + [((2 * OWN, PLANE + 128), BF)],
        xs,
        w_mine,
        w_other,
    )
    o_got = lax.ppermute(o_send, "filt", Z_SECOND)
    o_sum, o_send = call(
        halve_kernel, [((OWN, PLANE), F32), ((OWN, PLANE + 128), BF)], o_mine, o_first, o_got
    )
    o_got = lax.ppermute(o_send, "filt", Z_FIRST)
    (c_here,) = call(join_kernel, [((128, PLANE), BF)], *cots)

    r_send, r_cross, r_keep = call(
        split_xlo_kernel, [((CODED, 128), BF)] * 2 + [((PIECE + 8, 128), F32)], keep, r_core
    )
    r_far = lax.ppermute(r_send, ("filt", "space"), crossing(8, 8))
    r_near = lax.ppermute(r_cross, ("filt", "space"), crossing(0, 2))
    c_chip = lax.ppermute(c_here, "space", CORE)
    c_far = lax.ppermute(c_here, "space", BESIDE)

    (mine_y,) = call(code_kernel, [((CODED, 128), BF)], r_keep, r_near, r_far)
    y1, y3, y2 = (lax.ppermute(mine_y, "space", along_y(-r)) for r in (1, 3, 2))
    factor = float((16 * PLANE) ** -0.5)
    (piece,) = call(
        functools.partial(piece_kernel, factor=factor), [((CODED, 128), BF)], mine_y, y1, y2, y3
    )

    (wide_bias,) = call(bias_kernel, [((OWN, 1), F32)], bias.reshape(1, OWN))

    g_mine, g_theirs = call(
        input_grad_kernel,
        [((OWN, PLANE), F32), ((OWN, PLANE + 128), BF)],
        c_chip,
        c_far,
        *cots,
        w_mine,
        w_other,
        scratch=[pltpu.VMEM((9 * 128, PLANE), BF)],
    )
    g_other = lax.ppermute(g_theirs, "filt", ACROSS)
    wide = [((OWN, PLANE), F32)] * 2
    output, grad_inputs = call(
        sums_kernel,
        wide,
        o_sum,
        o_got,
        wide_bias,
        g_mine,
        g_other,
        scratch=[pltpu.VMEM(*v) for v in wide] + [pltpu.SemaphoreType.DMA((2,))],
        out_space=pl.BlockSpec(memory_space=pltpu.HBM),
    )

    piece_far = lax.ppermute(piece, "space", XLO)
    got_near = lax.ppermute(piece, "space", CORE)
    got_far = lax.ppermute(piece_far, "space", CORE)
    decoded = [((PIECE, 256), F32)]
    (mine,) = call(decode_kernel, decoded, piece)
    (mine_far,) = call(decode_kernel, decoded, piece_far)
    grad = ((9, 96, 256), F32)
    scratch = [pltpu.VMEM((PIECE, 256), F32), pltpu.SemaphoreType.DMA((5,))]
    hbm = pl.BlockSpec(memory_space=pltpu.HBM)
    half_done, grad_bias = call(
        first_kernel,
        [grad, ((1, OWN), F32)],
        mine,
        piece,
        got_near,
        scratch=scratch + [pltpu.VMEM((1, OWN), F32), pltpu.SemaphoreType.DMA],
        out_space=hbm,
    )
    (grad_weight,) = call(
        second_kernel, [grad], mine_far, got_far, half_done, scratch=scratch, out_space=hbm, over=2
    )
    return (
        output[None],
        grad_inputs[None],
        grad_weight.reshape(3, 3, 3, OWN, 256),
        grad_bias.reshape(OWN),
    )


def solution(mesh):
    placed = (
        P("space", "filt", None),
        P(None, None, None, "filt", None),
        P("filt"),
        P("space", "filt", None),
    )
    return jax.shard_map(
        step,
        mesh=mesh,
        in_specs=placed,
        out_specs=(
            P("space", "filt", None),
            P("space", "filt", None),
            P(None, None, None, "filt", None),
            P("filt"),
        ),
        check_vma=False,
    )
```

```python
import functools

import jax
import jax.numpy as jnp
from jax import lax
from jax.experimental import pallas as pl
from jax.experimental.pallas import tpu as pltpu
from jax.sharding import PartitionSpec as P


ROWS = 32
WIDE = 64
PLANE = ROWS * WIDE
OWN = 32
TAPS = 9 * OWN
HALF = 3 * TAPS
PIECE = HALF // 2
PART = 5 * 96
CODED = PIECE + 16
POWER = 15.0
TOP = 120.0
BF = jnp.bfloat16
F32 = jnp.float32

VM = pl.BlockSpec(memory_space=pltpu.VMEM)
PARAMS = pltpu.CompilerParams(vmem_limit_bytes=48 * 1024 * 1024)


def along_z(step):
    return [(f, ((f // 2 + step) % 4) * 2 + f % 2) for f in range(8)]


Z_FIRST = [(f, f ^ 2) for f in range(8)]
Z_SECOND = [(f, f ^ 6) for f in range(8)]
ACROSS = [(f, f ^ 1) for f in range(8)]
BESIDE = [
    (f * 16 + s, (f ^ 2) * 16 + s if s in (0, 15) else f * 16 + (s + 1 if s & 1 else s - 1))
    for f in range(8)
    for s in range(16)
]
CORE = [(s, s ^ 1) for s in range(16)]
XLO = [(s, s ^ 8) for s in range(16)]


def along_y(step):
    return [(s, (s & 9) | ((((s >> 1) + step) & 3) << 1)) for s in range(16)]


def crossing(flip, idle):
    return [
        (f * 16 + s, (f ^ 1) * 16 + (s ^ flip) if s & 1 else f * 16 + (s ^ idle))
        for f in range(8)
        for s in range(16)
    ]


def columns(shape):
    return lax.broadcasted_iota(jnp.int32, shape, 1) & (WIDE - 1)


def lanes(shape):
    return lax.broadcasted_iota(jnp.int32, shape, 1)


def select_kernel(w_hbm, x_hbm, c_hbm, mine_ref, theirs_ref, x_out, c_out, w_ref, sems):
    copies = [
        pltpu.make_async_copy(a, b, sems.at[i])
        for i, (a, b) in enumerate(((w_hbm, w_ref), (x_hbm, x_out), (c_hbm, c_out)))
    ]
    for copy in copies:
        copy.start()
    filt = lax.axis_index("filt")
    z, xh = filt // 2, filt % 2
    src = lax.broadcasted_iota(jnp.int32, (256, 256), 0)
    lane = lax.broadcasted_iota(jnp.int32, (256, 256), 1)
    side, turn, chan = lane >> 7, (lane >> 5) & 3, lane & 31
    want = ((z + turn) & 3) * 64 + ((xh + side) & 1) * 32 + chan
    pick = jnp.where(src == want, 1.0, 0.0).astype(BF)
    for copy in copies:
        copy.wait()
    got = jnp.dot(w_ref[...], pick, preferred_element_type=F32).astype(BF)
    mine_ref[...] = got[:, :128]
    even = (lax.axis_index("space") & 1) == 0
    theirs_ref[...] = jnp.where(even, got[:PART, 128:], got[864 - PART :, 128:])


def join_kernel(*refs):
    *parts, out_ref = refs
    at = 0
    for ref in parts:
        out_ref[at : at + ref.shape[0], :] = ref[...]
        at += ref.shape[0]


def join_w_kernel(near_ref, far_ref, out_ref):
    even = (lax.axis_index("space") & 1) == 0
    near, far = near_ref[...], far_ref[...]
    out_ref[:PART, :] = jnp.where(even, near, far)
    out_ref[PART:, :] = jnp.where(even, far, near)[2 * PART - 864 :]


def forward_kernel(xs_ref, wa_ref, wb_ref, mine_ref, first_ref, send_ref):
    rhs = jnp.concatenate([xs_ref[0, :TAPS, :], xs_ref[1, :TAPS, :]], axis=0)
    parts = []
    for kh in range(3):
        lhs = jnp.concatenate(
            [w[(kd * 3 + kh) * 96 : (kd * 3 + kh) * 96 + 96, :] for w in (wa_ref, wb_ref) for kd in range(3)],
            axis=0,
        )
        parts.append(
            lax.dot_general(lhs, rhs, (((0,), (0,)), ((), ())), preferred_element_type=F32)
        )
    lane = lanes((128, PLANE))
    total = (
        parts[1]
        + jnp.where(lane < WIDE, 0.0, pltpu.roll(parts[0], WIDE, 1))
        + jnp.where(lane >= PLANE - WIDE, 0.0, pltpu.roll(parts[2], PLANE - WIDE, 1))
    )
    even = ((lax.axis_index("filt") // 2) & 1) == 0
    near, across, far = (total[r * 32 : r * 32 + 32] for r in (1, 2, 3))
    mine_ref[...] = total[:32]
    first_ref[...] = jnp.where(even, near, far)
    write_rows(send_ref, jnp.concatenate([jnp.where(even, far, near), across], axis=0))


def row_shifts(wide):
    lane = lanes(wide.shape)
    turned = pltpu.roll(wide, PLANE - WIDE, 1)
    up = jnp.where(lane >= PLANE - WIDE, 0.0, turned)
    down = jnp.where(lane < WIDE, 0.0, pltpu.roll(wide, WIDE, 1))
    return up.astype(BF), wide.astype(BF), down.astype(BF)


def beside():
    space = lax.axis_index("space")
    inside = jnp.logical_and(space != 0, space != 15).astype(F32)
    return inside, (space & 1) == 0


def kernel_grad_kernel(chip_ref, here_ref, far_ref, c0, c1, c2, c3, xs_ref, keep_ref, send_ref, cs_ref):
    core = lax.axis_index("space") & 1
    col = columns((64, PLANE))
    inside, even = beside()
    for ref, kd in ((chip_ref, jnp.where(even, 2, 0)), (here_ref, 1), (far_ref, jnp.where(even, 0, 2))):
        wide = ref[...].astype(F32)
        if ref is far_ref:
            wide = wide * inside
        left = jnp.where(col == 0, 0.0, pltpu.roll(wide, 1, 1))
        right = jnp.where(col == WIDE - 1, 0.0, pltpu.roll(wide, PLANE - 1, 1))
        for kw, part in enumerate((left, wide, right)):
            rows = pl.ds(pl.multiple_of((kd * 3 + kw) * OWN, OWN), OWN)
            narrow = part.astype(BF)
            xs_ref[0, rows, :] = narrow[:OWN]
            xs_ref[1, rows, :] = narrow[OWN:]
    xs_ref[:, TAPS:, :] = jnp.ones((2, 16, PLANE), BF)
    for r, ref in enumerate((c0, c1, c2, c3)):
        for kh, part in enumerate(row_shifts(ref[...].astype(F32))):
            cs_ref[kh * 128 + r * 32 : kh * 128 + r * 32 + 32, :] = part
    for slot, ref in enumerate((keep_ref, send_ref)):
        got = lax.dot_general(
            xs_ref[core ^ slot], cs_ref[...], (((1,), (1,)), ((), ())), preferred_element_type=F32
        )
        for kh in range(3):
            ref[kh * TAPS : (kh + 1) * TAPS, :] = got[:TAPS, kh * 128 : kh * 128 + 128]
        ref[HALF:, :] = got[TAPS : TAPS + 8, 128:256]


def input_grad_kernel(chip_ref, far_ref, c0, c1, c2, c3, wa_ref, wb_ref, mine_ref, theirs_ref, cs_ref):
    inside, even = beside()
    for r, ref in enumerate((c0, c1, c2, c3)):
        rows = slice(r * 32, r * 32 + 32)
        planes = (
            chip_ref[rows, :].astype(F32),
            ref[...].astype(F32),
            far_ref[rows, :].astype(F32) * inside,
        )
        for kd, wide in enumerate(planes):
            for kh, part in enumerate(row_shifts(wide)):
                at = (kd * 3 + kh) * 128 + r * 32
                cs_ref[at : at + 32, :] = part

    def taps(w, kd, kh):
        ahead, here, behind = (w[(k * 3 + kh) * 96 : (k * 3 + kh) * 96 + 96, :] for k in range(3))
        if kd == 1:
            return here
        first, second = (ahead, behind) if kd == 0 else (behind, ahead)
        return jnp.where(even, first, second)

    lhs = jnp.concatenate(
        [
            jnp.concatenate([taps(w, kd, kh) for kd in range(3) for kh in range(3)], axis=1)
            for w in (wa_ref, wb_ref)
        ],
        axis=0,
    )
    got = jnp.dot(lhs, cs_ref[...], preferred_element_type=F32)
    col = columns((OWN, PLANE))
    for h in range(2):
        base = h * 96
        part = (
            got[base + 32 : base + 64]
            + jnp.where(col == WIDE - 1, 0.0, pltpu.roll(got[base : base + 32], PLANE - 1, 1))
            + jnp.where(col == 0, 0.0, pltpu.roll(got[base + 64 : base + 96], 1, 1))
        )
        if h == 0:
            mine_ref[...] = part
        else:
            write_rows(theirs_ref, part)


def encode(wide):
    size = jnp.abs(wide)
    scale = jnp.max(jnp.max(size, axis=1, keepdims=True), axis=0, keepdims=True)
    scale = jnp.maximum(scale, 1e-30).astype(BF).astype(F32)
    coded = jnp.exp2(jnp.log2(size * (1.0 / scale)) * POWER + TOP)
    return jnp.where(wide < 0, -coded, coded).astype(BF), scale


def decode(coded, scale):
    wide = coded.astype(F32)
    size = scale * jnp.exp2((jnp.log2(jnp.abs(wide)) - TOP) * (1.0 / POWER))
    return jnp.where(wide < 0, -size, size)


def write_coded(out_ref, wide, bias):
    coded, scale = encode(wide)
    high = bias.astype(BF).astype(F32)
    low = bias - high
    row = lax.broadcasted_iota(jnp.int32, (16, 128), 0)
    tail = jnp.where(row == 0, scale, jnp.where(row == 1, high, jnp.where(row == 2, low, 0.0)))
    out_ref[:PIECE, :] = coded
    out_ref[PIECE:, :] = tail.astype(BF)


def read_tail(tail):
    return tail[1:2, :] + tail[2:3, :]


def read_coded(ref):
    tail = ref[PIECE:CODED, :].astype(F32)
    return decode(ref[:PIECE, :], tail[0:1, 0:1]), read_tail(tail)


def write_rows(out_ref, wide):
    out_ref[:, :PLANE], scale = encode(wide)
    out_ref[:, PLANE:] = jnp.broadcast_to(scale, (wide.shape[0], 128)).astype(BF)


def read_rows(coded):
    return decode(coded[:, :PLANE], coded[0:1, PLANE : PLANE + 1].astype(F32))


def split_xlo_kernel(keep_ref, got_ref, send_out, cross_out, keep_out):
    xlo = lax.axis_index("space") // 8
    bias = keep_ref[HALF:, :] + got_ref[HALF:, :]
    send, keep = (
        keep_ref[rows, :] + got_ref[rows, :]
        for rows in (pl.ds(pl.multiple_of(at, 8), PIECE) for at in ((1 - xlo) * PIECE, xlo * PIECE))
    )
    write_coded(send_out, send, bias[:1])
    write_coded(cross_out, keep, bias[:1])
    keep_out[:PIECE, :] = keep
    keep_out[PIECE:, :] = bias


def code_kernel(keep_ref, near_ref, far_ref, out_ref):
    even = (lax.axis_index("space") & 1) == 0
    near, far = read_coded(near_ref), read_coded(far_ref)
    write_coded(
        out_ref,
        jnp.where(even, keep_ref[:PIECE, :], near[0]) + far[0],
        jnp.where(even, keep_ref[PIECE : PIECE + 1, :], near[1]) + far[1],
    )


def piece_kernel(own_ref, y1_ref, y2_ref, y3_ref, out_ref, *, factor):
    own, y1, y2, y3 = (read_coded(r) for r in (own_ref, y1_ref, y2_ref, y3_ref))
    wide, bias = ((own[i] + y2[i]) + (y1[i] + y3[i]) for i in range(2))
    z = lax.axis_index("filt") // 2
    write_coded(out_ref, pltpu.roll(wide * factor, z * 32, 1), bias * factor)


def side_of(swap):
    return (lax.axis_index("filt") ^ lax.axis_index("space") ^ swap) & 1


def spread(wide, side):
    first, second, third, fourth = (
        pltpu.roll(wide, ((side + j) & 3) * 32, 1) for j in range(4)
    )
    low = lanes(wide.shape) < 64
    return jnp.where(low, first, second), jnp.where(low, third, fourth)


def decode_kernel(own_ref, out_ref):
    out_ref[:, :128], out_ref[:, 128:] = spread(read_coded(own_ref)[0], side_of(0))


def write_half(turn, own_ref, got_ref, grad_hbm, rows_ref, sems):
    wide, bias = read_coded(got_ref)
    side = side_of(1)
    theirs = ((lanes((PIECE, 128)) >> 5) & 1) == side
    for t, part in enumerate(spread(wide, side)):
        cols = slice(t * 128, t * 128 + 128)
        rows_ref[:, cols] = jnp.where(theirs, part, own_ref[:, cols])
    half = (lax.axis_index("space") // 8) ^ turn
    spans = []
    for j in range(4):
        block = j + 5 * half
        to = lax.rem(block, 3) * 3 + lax.div(block, 3)
        spans.append((half * 48 + j * 96, 96, to, 0))
    spans.append(((1 - half) * 384, 48, 4, half * 48))
    copies = [
        pltpu.make_async_copy(
            rows_ref.at[pl.ds(pl.multiple_of(at, 16), size), :],
            grad_hbm.at[to, pl.ds(row if isinstance(row, int) else pl.multiple_of(row, 16), size), :],
            sems.at[i],
        )
        for i, (at, size, to, row) in enumerate(spans)
    ]
    for copy in copies:
        copy.start()
    return bias[:, :OWN], copies


def first_kernel(own_ref, piece_ref, got_ref, grad_hbm, bias_hbm, rows_ref, sems, bias_ref, bias_sem):
    bias, copies = write_half(0, own_ref, got_ref, grad_hbm, rows_ref, sems)
    core = lax.axis_index("space") & 1
    own_bias = read_tail(piece_ref[PIECE:CODED, :].astype(F32))[:, :OWN]
    bias_ref[...] = jnp.where(core == 0, own_bias, bias)
    copies.append(pltpu.make_async_copy(bias_ref, bias_hbm, bias_sem))
    copies[-1].start()
    for copy in copies:
        copy.wait()


def second_kernel(own_ref, got_ref, _, grad_hbm, rows_ref, sems):
    for copy in write_half(1, own_ref, got_ref, grad_hbm, rows_ref, sems)[1]:
        copy.wait()


def widen_kernel(ref, out):
    out[...] = ref[...].astype(F32)


def bias_kernel(ref, out):
    row = lax.broadcasted_iota(jnp.int32, (OWN, OWN), 0)
    col = lax.broadcasted_iota(jnp.int32, (OWN, OWN), 1)
    out[...] = jnp.sum(jnp.where(row == col, ref[...], 0.0), axis=1, keepdims=True)


def halve_kernel(mine_ref, first_ref, got_ref, sum_ref, send_ref):
    got = read_rows(got_ref[...])
    sum_ref[...] = mine_ref[...] + got[:OWN]
    write_rows(send_ref, first_ref[...] + got[OWN:])


def sums_kernel(mine_ref, got_ref, bias_ref, near_ref, theirs_ref, out_hbm, grad_hbm, out_ref, grad_ref, sems):
    copies = [
        pltpu.make_async_copy(out_ref, out_hbm, sems.at[0]),
        pltpu.make_async_copy(grad_ref, grad_hbm, sems.at[1]),
    ]
    out_ref[...] = mine_ref[...] + read_rows(got_ref[...]) + bias_ref[...]
    copies[0].start()
    grad_ref[...] = near_ref[...] + read_rows(theirs_ref[...])
    copies[1].start()
    for copy in copies:
        copy.wait()


def call(kernel, outs, *args, scratch=(), space=VM, out_space=VM, over=None):
    return pl.pallas_call(
        kernel,
        out_shape=[jax.ShapeDtypeStruct(s, d) for s, d in outs],
        in_specs=[space if i != over else out_space for i in range(len(args))],
        input_output_aliases={} if over is None else {over: 0},
        out_specs=[out_space] * len(outs),
        scratch_shapes=list(scratch),
        compiler_params=PARAMS,
    )(*args)


def step(inputs, weight, bias, cotangent):
    x_own = inputs[0]
    c_own = cotangent[0]

    x_other = lax.ppermute(x_own, "filt", ACROSS)
    c1, c3, c2 = (lax.ppermute(c_own, "filt", along_z(-r)) for r in (1, 3, 2))
    w_mine, w_theirs, x_near, c_near = call(
        select_kernel,
        [((864, 128), BF), ((PART, 128), BF), ((OWN, PLANE), BF), ((OWN, PLANE), BF)],
        *(pltpu.with_memory_space_constraint(v, pltpu.HBM) for v in (weight.reshape(864, 256), x_own, c_own)),
        scratch=[pltpu.VMEM((864, 256), BF), pltpu.SemaphoreType.DMA((3,))],
        space=pl.BlockSpec(memory_space=pltpu.HBM),
    )
    w_half = lax.ppermute(w_theirs, "filt", ACROSS)
    w_rest = lax.ppermute(w_half, "space", CORE)
    (w_other,) = call(join_w_kernel, [((864, 128), BF)], w_half, w_rest)
    cots = [c_near, c1, c2, c3]

    (x_here,) = call(join_kernel, [((64, PLANE), BF)], x_near, x_other)
    x_chip = lax.ppermute(x_here, "space", CORE)
    x_far = lax.ppermute(x_here, ("filt", "space"), BESIDE)

    xs, keep, send = call(
        kernel_grad_kernel,
        [((2, TAPS + 16, PLANE), BF)] + [((HALF + 8, 128), F32)] * 2,
        x_chip,
        x_here,
        x_far,
        *cots,
        scratch=[pltpu.VMEM((384, PLANE), BF)],
    )
    r_core = lax.ppermute(send, "space", CORE)
    o_mine, o_first, o_send = call(
        forward_kernel,
        [((OWN, PLANE), F32)] * 2 + [((2 * OWN, PLANE + 128), BF)],
        xs,
        w_mine,
        w_other,
    )
    o_got = lax.ppermute(o_send, "filt", Z_SECOND)
    o_sum, o_send = call(
        halve_kernel, [((OWN, PLANE), F32), ((OWN, PLANE + 128), BF)], o_mine, o_first, o_got
    )
    o_got = lax.ppermute(o_send, "filt", Z_FIRST)
    (c_here,) = call(join_kernel, [((128, PLANE), BF)], *cots)

    r_send, r_cross, r_keep = call(
        split_xlo_kernel, [((CODED, 128), BF)] * 2 + [((PIECE + 8, 128), F32)], keep, r_core
    )
    r_far = lax.ppermute(r_send, ("filt", "space"), crossing(8, 8))
    r_near = lax.ppermute(r_cross, ("filt", "space"), crossing(0, 2))
    c_chip = lax.ppermute(c_here, "space", CORE)
    c_far = lax.ppermute(c_here, ("filt", "space"), BESIDE)

    (mine_y,) = call(code_kernel, [((CODED, 128), BF)], r_keep, r_near, r_far)
    y1, y3, y2 = (lax.ppermute(mine_y, "space", along_y(-r)) for r in (1, 3, 2))
    factor = float((16 * PLANE) ** -0.5)
    (piece,) = call(
        functools.partial(piece_kernel, factor=factor), [((CODED, 128), BF)], mine_y, y1, y2, y3
    )

    (row_bias,) = call(widen_kernel, [((1, OWN), F32)], bias.reshape(1, OWN))
    (wide_bias,) = call(bias_kernel, [((OWN, 1), F32)], row_bias)

    g_mine, g_theirs = call(
        input_grad_kernel,
        [((OWN, PLANE), F32), ((OWN, PLANE + 128), BF)],
        c_chip,
        c_far,
        *cots,
        w_mine,
        w_other,
        scratch=[pltpu.VMEM((9 * 128, PLANE), BF)],
    )
    g_other = lax.ppermute(g_theirs, "filt", ACROSS)
    wide = [((OWN, PLANE), F32)] * 2
    output, grad_inputs = call(
        sums_kernel,
        wide,
        o_sum,
        o_got,
        wide_bias,
        g_mine,
        g_other,
        scratch=[pltpu.VMEM(*v) for v in wide] + [pltpu.SemaphoreType.DMA((2,))],
        out_space=pl.BlockSpec(memory_space=pltpu.HBM),
    )

    piece_far = lax.ppermute(piece, "space", XLO)
    got_near = lax.ppermute(piece, "space", CORE)
    got_far = lax.ppermute(piece_far, "space", CORE)
    decoded = [((PIECE, 256), F32)]
    (mine,) = call(decode_kernel, decoded, piece)
    (mine_far,) = call(decode_kernel, decoded, piece_far)
    grad = ((9, 96, 256), F32)
    scratch = [pltpu.VMEM((PIECE, 256), F32), pltpu.SemaphoreType.DMA((5,))]
    hbm = pl.BlockSpec(memory_space=pltpu.HBM)
    half_done, grad_bias = call(
        first_kernel,
        [grad, ((1, OWN), F32)],
        mine,
        piece,
        got_near,
        scratch=scratch + [pltpu.VMEM((1, OWN), F32), pltpu.SemaphoreType.DMA],
        out_space=hbm,
    )
    (grad_weight,) = call(
        second_kernel, [grad], mine_far, got_far, half_done, scratch=scratch, out_space=hbm, over=2
    )
    return (
        output[None],
        grad_inputs[None],
        grad_weight.reshape(3, 3, 3, OWN, 256),
        grad_bias.reshape(OWN),
    )


def solution(mesh):
    placed = (
        P("space", "filt", None),
        P(None, None, None, "filt", None),
        P("filt"),
        P("space", "filt", None),
    )
    return jax.shard_map(
        step,
        mesh=mesh,
        in_specs=placed,
        out_specs=(
            P("space", "filt", None),
            P("space", "filt", None),
            P(None, None, None, "filt", None),
            P("filt"),
        ),
        check_vma=False,
    )
```

```python
import functools

import jax
import jax.numpy as jnp
from jax import lax
from jax.experimental import pallas as pl
from jax.experimental.pallas import tpu as pltpu
from jax.sharding import PartitionSpec as P


ROWS = 32
WIDE = 64
PLANE = ROWS * WIDE
OWN = 32
TAPS = 9 * OWN
HALF = 3 * TAPS
PIECE = HALF // 2
PART = 5 * 96
CODED = PIECE + 16
POWER = 15.0
TOP = 120.0
BF = jnp.bfloat16
F32 = jnp.float32

VM = pl.BlockSpec(memory_space=pltpu.VMEM)
PARAMS = pltpu.CompilerParams(vmem_limit_bytes=48 * 1024 * 1024)


def along_z(step):
    return [(f, ((f // 2 + step) % 4) * 2 + f % 2) for f in range(8)]


Z_FIRST = [(f, f ^ 2) for f in range(8)]
Z_SECOND = [(f, f ^ 6) for f in range(8)]
ACROSS = [(f, f ^ 1) for f in range(8)]
BESIDE = [
    (f * 16 + s, (f ^ 2) * 16 + s if s in (0, 15) else f * 16 + (s + 1 if s & 1 else s - 1))
    for f in range(8)
    for s in range(16)
]
CORE = [(s, s ^ 1) for s in range(16)]
XLO = [(s, s ^ 8) for s in range(16)]


def along_y(step):
    return [(s, (s & 9) | ((((s >> 1) + step) & 3) << 1)) for s in range(16)]


def crossing(flip, idle):
    return [
        (f * 16 + s, (f ^ 1) * 16 + (s ^ flip) if s & 1 else f * 16 + (s ^ idle))
        for f in range(8)
        for s in range(16)
    ]


def columns(shape):
    return lax.broadcasted_iota(jnp.int32, shape, 1) & (WIDE - 1)


def lanes(shape):
    return lax.broadcasted_iota(jnp.int32, shape, 1)


def select_kernel(w_hbm, x_hbm, c_hbm, mine_ref, theirs_ref, x_out, c_out, w_ref, sems):
    copies = [
        pltpu.make_async_copy(a, b, sems.at[i])
        for i, (a, b) in enumerate(((w_hbm, w_ref), (x_hbm, x_out), (c_hbm, c_out)))
    ]
    for copy in copies:
        copy.start()
    filt = lax.axis_index("filt")
    z, xh = filt // 2, filt % 2
    src = lax.broadcasted_iota(jnp.int32, (256, 256), 0)
    lane = lax.broadcasted_iota(jnp.int32, (256, 256), 1)
    side, turn, chan = lane >> 7, (lane >> 5) & 3, lane & 31
    want = ((z + turn) & 3) * 64 + ((xh + side) & 1) * 32 + chan
    pick = jnp.where(src == want, 1.0, 0.0).astype(BF)
    for copy in copies:
        copy.wait()
    got = jnp.dot(w_ref[...], pick, preferred_element_type=F32).astype(BF)
    mine_ref[...] = got[:, :128]
    even = (lax.axis_index("space") & 1) == 0
    theirs_ref[...] = jnp.where(even, got[:PART, 128:], got[864 - PART :, 128:])


def join_kernel(*refs):
    *parts, out_ref = refs
    at = 0
    for ref in parts:
        out_ref[at : at + ref.shape[0], :] = ref[...]
        at += ref.shape[0]


def join_w_kernel(near_ref, far_ref, out_ref):
    even = (lax.axis_index("space") & 1) == 0
    near, far = near_ref[...], far_ref[...]
    out_ref[:PART, :] = jnp.where(even, near, far)
    out_ref[PART:, :] = jnp.where(even, far, near)[2 * PART - 864 :]


def forward_kernel(xs_ref, wa_ref, wb_ref, mine_ref, first_ref, send_ref):
    rhs = jnp.concatenate([xs_ref[0, :TAPS, :], xs_ref[1, :TAPS, :]], axis=0)
    lhs = jnp.concatenate(
        [
            jnp.concatenate(
                [w[(kd * 3 + kh) * 96 : (kd * 3 + kh) * 96 + 96, :] for w in (wa_ref, wb_ref) for kd in range(3)],
                axis=0,
            )
            for kh in range(3)
        ],
        axis=1,
    )
    got = lax.dot_general(lhs, rhs, (((0,), (0,)), ((), ())), preferred_element_type=F32)
    parts = [got[kh * 128 : kh * 128 + 128] for kh in range(3)]
    high = (lanes((128, PLANE)) & 127) >= WIDE
    later, earlier = beside_tiles(parts[0])[0], beside_tiles(parts[2])[1]
    total = parts[1] + half_turn(jnp.where(high, later + parts[2], parts[0] + earlier))
    even = ((lax.axis_index("filt") // 2) & 1) == 0
    near, across, far = (total[r * 32 : r * 32 + 32] for r in (1, 2, 3))
    mine_ref[...] = total[:32]
    first_ref[...] = jnp.where(even, near, far)
    write_rows(send_ref, jnp.concatenate([jnp.where(even, far, near), across], axis=0))


def half_turn(wide):
    return jnp.concatenate(
        [pltpu.roll(wide[:, at : at + 128], WIDE, 1) for at in range(0, PLANE, 128)], axis=1
    )


def beside_tiles(wide):
    none = jnp.zeros((wide.shape[0], 128), wide.dtype)
    return (
        jnp.concatenate([none, wide[:, :-128]], axis=1),
        jnp.concatenate([wide[:, 128:], none], axis=1),
    )


def row_shifts(wide):
    low = (lanes(wide.shape) & 127) < WIDE
    turned = half_turn(wide)
    later, earlier = beside_tiles(turned)
    return jnp.where(low, turned, earlier), wide, jnp.where(low, later, turned)


def beside():
    space = lax.axis_index("space")
    inside = jnp.logical_and(space != 0, space != 15).astype(F32)
    return inside, (space & 1) == 0


def kernel_grad_kernel(chip_ref, here_ref, far_ref, c0, c1, c2, c3, xs_ref, keep_ref, send_ref, cs_ref):
    col = columns((64, PLANE))
    inside, even = beside()
    for ref, kd in ((chip_ref, jnp.where(even, 2, 0)), (here_ref, 1), (far_ref, jnp.where(even, 0, 2))):
        wide = ref[...]
        if ref is far_ref:
            wide = wide * inside.astype(BF)
        left = jnp.where(col == 0, 0.0, pltpu.roll(wide, 1, 1))
        right = jnp.where(col == WIDE - 1, 0.0, pltpu.roll(wide, PLANE - 1, 1))
        for kw, part in enumerate((left, wide, right)):
            rows = pl.ds(pl.multiple_of((kd * 3 + kw) * OWN, OWN), OWN)
            narrow = part.astype(BF)
            xs_ref[0, rows, :] = narrow[:OWN]
            xs_ref[1, rows, :] = narrow[OWN:]
    xs_ref[:, TAPS:, :] = jnp.ones((2, 16, PLANE), BF)
    for r, ref in enumerate((c0, c1, c2, c3)):
        for kh, part in enumerate(row_shifts(ref[...])):
            cs_ref[kh * 128 + r * 32 : kh * 128 + r * 32 + 32, :] = part
    got = lax.dot_general(
        xs_ref[...].reshape(2 * (TAPS + 16), PLANE),
        cs_ref[...],
        (((1,), (1,)), ((), ())),
        preferred_element_type=F32,
    )
    first, second = got[: TAPS + 16], got[TAPS + 16 :]
    for ref, half in ((keep_ref, jnp.where(even, first, second)), (send_ref, jnp.where(even, second, first))):
        for kh in range(3):
            ref[kh * TAPS : (kh + 1) * TAPS, :] = half[:TAPS, kh * 128 : kh * 128 + 128]
        ref[HALF:, :] = half[TAPS : TAPS + 8, 128:256]


def input_grad_kernel(chip_ref, far_ref, c0, c1, c2, c3, wa_ref, wb_ref, mine_ref, theirs_ref, cs_ref):
    inside, even = beside()
    for r, ref in enumerate((c0, c1, c2, c3)):
        rows = slice(r * 32, r * 32 + 32)
        planes = (
            chip_ref[rows, :],
            ref[...],
            far_ref[rows, :] * inside.astype(BF),
        )
        for kd, wide in enumerate(planes):
            for kh, part in enumerate(row_shifts(wide)):
                at = (kd * 3 + kh) * 128 + r * 32
                cs_ref[at : at + 32, :] = part

    def taps(w, kd, kh):
        ahead, here, behind = (w[(k * 3 + kh) * 96 : (k * 3 + kh) * 96 + 96, :] for k in range(3))
        if kd == 1:
            return here
        first, second = (ahead, behind) if kd == 0 else (behind, ahead)
        return jnp.where(even, first, second)

    lhs = jnp.concatenate(
        [
            jnp.concatenate([taps(w, kd, kh) for kd in range(3) for kh in range(3)], axis=1)
            for w in (wa_ref, wb_ref)
        ],
        axis=0,
    )
    got = jnp.dot(lhs, cs_ref[...], preferred_element_type=F32)
    col = columns((OWN, PLANE))
    for h in range(2):
        base = h * 96
        part = (
            got[base + 32 : base + 64]
            + jnp.where(col == WIDE - 1, 0.0, pltpu.roll(got[base : base + 32], PLANE - 1, 1))
            + jnp.where(col == 0, 0.0, pltpu.roll(got[base + 64 : base + 96], 1, 1))
        )
        if h == 0:
            mine_ref[...] = part
        else:
            write_rows(theirs_ref, part)


def encode(wide):
    size = jnp.abs(wide)
    scale = jnp.max(jnp.max(size, axis=1, keepdims=True), axis=0, keepdims=True)
    scale = jnp.maximum(scale, 1e-37).astype(BF).astype(F32)
    coded = jnp.exp2(jnp.log2(size * (1.0 / scale)) * POWER + TOP)
    return jnp.where(wide < 0, -coded, coded).astype(BF), scale


def decode(coded, scale):
    wide = coded.astype(F32)
    size = scale * jnp.exp2((jnp.log2(jnp.abs(wide)) - TOP) * (1.0 / POWER))
    return jnp.where(wide < 0, -size, size)


def write_coded(out_ref, wide, bias):
    coded, scale = encode(wide)
    high = bias.astype(BF).astype(F32)
    low = bias - high
    row = lax.broadcasted_iota(jnp.int32, (16, 128), 0)
    tail = jnp.where(row == 0, scale, jnp.where(row == 1, high, jnp.where(row == 2, low, 0.0)))
    out_ref[:PIECE, :] = coded
    out_ref[PIECE:, :] = tail.astype(BF)


def read_tail(tail):
    return tail[1:2, :] + tail[2:3, :]


def read_coded(ref):
    tail = ref[PIECE:CODED, :].astype(F32)
    return decode(ref[:PIECE, :], tail[0:1, 0:1]), read_tail(tail)


def write_rows(out_ref, wide):
    out_ref[:, :PLANE], scale = encode(wide)
    out_ref[:, PLANE:] = jnp.broadcast_to(scale, (wide.shape[0], 128)).astype(BF)


def read_rows(coded):
    return decode(coded[:, :PLANE], coded[0:1, PLANE : PLANE + 1].astype(F32))


def split_xlo_kernel(keep_ref, got_ref, send_out, cross_out, keep_out):
    xlo = lax.axis_index("space") // 8
    bias = keep_ref[HALF:, :] + got_ref[HALF:, :]
    send, keep = (
        keep_ref[rows, :] + got_ref[rows, :]
        for rows in (pl.ds(pl.multiple_of(at, 8), PIECE) for at in ((1 - xlo) * PIECE, xlo * PIECE))
    )
    write_coded(send_out, send, bias[:1])
    write_coded(cross_out, keep, bias[:1])
    keep_out[:PIECE, :] = keep
    keep_out[PIECE:, :] = bias


def code_kernel(keep_ref, near_ref, far_ref, out_ref):
    even = (lax.axis_index("space") & 1) == 0
    near, far = read_coded(near_ref), read_coded(far_ref)
    write_coded(
        out_ref,
        jnp.where(even, keep_ref[:PIECE, :], near[0]) + far[0],
        jnp.where(even, keep_ref[PIECE : PIECE + 1, :], near[1]) + far[1],
    )


def piece_kernel(own_ref, y1_ref, y2_ref, y3_ref, out_ref, *, factor):
    own, y1, y2, y3 = (read_coded(r) for r in (own_ref, y1_ref, y2_ref, y3_ref))
    wide, bias = ((own[i] + y2[i]) + (y1[i] + y3[i]) for i in range(2))
    z = lax.axis_index("filt") // 2
    write_coded(out_ref, pltpu.roll(wide * factor, z * 32, 1), bias * factor)


def side_of(swap):
    return (lax.axis_index("filt") ^ lax.axis_index("space") ^ swap) & 1


def spread(wide, side):
    first, second, third, fourth = (
        pltpu.roll(wide, ((side + j) & 3) * 32, 1) for j in range(4)
    )
    low = lanes(wide.shape) < 64
    return jnp.where(low, first, second), jnp.where(low, third, fourth)


def decode_kernel(own_ref, out_ref):
    out_ref[:, :128], out_ref[:, 128:] = spread(read_coded(own_ref)[0], side_of(0))


def write_half(turn, own_ref, got_ref, grad_hbm, rows_ref, sems):
    wide, bias = read_coded(got_ref)
    side = side_of(1)
    theirs = ((lanes((PIECE, 128)) >> 5) & 1) == side
    for t, part in enumerate(spread(wide, side)):
        cols = slice(t * 128, t * 128 + 128)
        rows_ref[:, cols] = jnp.where(theirs, part, own_ref[:, cols])
    half = (lax.axis_index("space") // 8) ^ turn
    spans = []
    for j in range(4):
        block = j + 5 * half
        to = lax.rem(block, 3) * 3 + lax.div(block, 3)
        spans.append((half * 48 + j * 96, 96, to, 0))
    spans.append(((1 - half) * 384, 48, 4, half * 48))
    copies = [
        pltpu.make_async_copy(
            rows_ref.at[pl.ds(pl.multiple_of(at, 16), size), :],
            grad_hbm.at[to, pl.ds(row if isinstance(row, int) else pl.multiple_of(row, 16), size), :],
            sems.at[i],
        )
        for i, (at, size, to, row) in enumerate(spans)
    ]
    for copy in copies:
        copy.start()
    return bias[:, :OWN], copies


def first_kernel(
    own_ref, piece_ref, got_ref, sum_ref, sum_got_ref, wide_ref, near_ref, theirs_ref,
    grad_hbm, bias_hbm, out_hbm, gin_hbm, rows_ref, sems, bias_ref, out_ref, gin_ref, more,
):
    bias, copies = write_half(0, own_ref, got_ref, grad_hbm, rows_ref, sems)
    core = lax.axis_index("space") & 1
    own_bias = read_tail(piece_ref[PIECE:CODED, :].astype(F32))[:, :OWN]
    bias_ref[...] = jnp.where(core == 0, own_bias, bias)
    copies.append(pltpu.make_async_copy(bias_ref, bias_hbm, more.at[0]))
    copies[-1].start()
    out_ref[...] = sum_ref[...] + read_rows(sum_got_ref[...]) + wide_ref[...]
    copies.append(pltpu.make_async_copy(out_ref, out_hbm, more.at[1]))
    copies[-1].start()
    gin_ref[...] = near_ref[...] + read_rows(theirs_ref[...])
    copies.append(pltpu.make_async_copy(gin_ref, gin_hbm, more.at[2]))
    copies[-1].start()
    for copy in copies:
        copy.wait()


def second_kernel(own_ref, got_ref, _, grad_hbm, rows_ref, sems):
    for copy in write_half(1, own_ref, got_ref, grad_hbm, rows_ref, sems)[1]:
        copy.wait()


def widen_kernel(ref, out):
    out[...] = ref[...].astype(F32)


def bias_kernel(ref, out):
    row = lax.broadcasted_iota(jnp.int32, (OWN, OWN), 0)
    col = lax.broadcasted_iota(jnp.int32, (OWN, OWN), 1)
    out[...] = jnp.sum(jnp.where(row == col, ref[...], 0.0), axis=1, keepdims=True)


def halve_kernel(mine_ref, first_ref, got_ref, sum_ref, send_ref):
    got = read_rows(got_ref[...])
    sum_ref[...] = mine_ref[...] + got[:OWN]
    write_rows(send_ref, first_ref[...] + got[OWN:])


def call(kernel, outs, *args, scratch=(), space=VM, out_space=VM, over=None):
    return pl.pallas_call(
        kernel,
        out_shape=[jax.ShapeDtypeStruct(s, d) for s, d in outs],
        in_specs=[space if i != over else out_space for i in range(len(args))],
        input_output_aliases={} if over is None else {over: 0},
        out_specs=[out_space] * len(outs),
        scratch_shapes=list(scratch),
        compiler_params=PARAMS,
    )(*args)


def step(inputs, weight, bias, cotangent):
    x_own = inputs[0]
    c_own = cotangent[0]

    x_other = lax.ppermute(x_own, "filt", ACROSS)
    c1, c3, c2 = (lax.ppermute(c_own, "filt", along_z(-r)) for r in (1, 3, 2))
    w_mine, w_theirs, x_near, c_near = call(
        select_kernel,
        [((864, 128), BF), ((PART, 128), BF), ((OWN, PLANE), BF), ((OWN, PLANE), BF)],
        *(pltpu.with_memory_space_constraint(v, pltpu.HBM) for v in (weight.reshape(864, 256), x_own, c_own)),
        scratch=[pltpu.VMEM((864, 256), BF), pltpu.SemaphoreType.DMA((3,))],
        space=pl.BlockSpec(memory_space=pltpu.HBM),
    )
    w_half = lax.ppermute(w_theirs, "filt", ACROSS)
    w_rest = lax.ppermute(w_half, "space", CORE)
    (w_other,) = call(join_w_kernel, [((864, 128), BF)], w_half, w_rest)
    cots = [c_near, c1, c2, c3]

    (x_here,) = call(join_kernel, [((64, PLANE), BF)], x_near, x_other)
    x_chip = lax.ppermute(x_here, "space", CORE)
    x_far = lax.ppermute(x_here, ("filt", "space"), BESIDE)

    xs, keep, send = call(
        kernel_grad_kernel,
        [((2, TAPS + 16, PLANE), BF)] + [((HALF + 8, 128), F32)] * 2,
        x_chip,
        x_here,
        x_far,
        *cots,
        scratch=[pltpu.VMEM((384, PLANE), BF)],
    )
    r_core = lax.ppermute(send, "space", CORE)
    o_mine, o_first, o_send = call(
        forward_kernel,
        [((OWN, PLANE), F32)] * 2 + [((2 * OWN, PLANE + 128), BF)],
        xs,
        w_mine,
        w_other,
    )
    o_got = lax.ppermute(o_send, "filt", Z_SECOND)
    o_sum, o_send = call(
        halve_kernel, [((OWN, PLANE), F32), ((OWN, PLANE + 128), BF)], o_mine, o_first, o_got
    )
    o_got = lax.ppermute(o_send, "filt", Z_FIRST)
    (c_here,) = call(join_kernel, [((128, PLANE), BF)], *cots)

    r_send, r_cross, r_keep = call(
        split_xlo_kernel, [((CODED, 128), BF)] * 2 + [((PIECE + 8, 128), F32)], keep, r_core
    )
    r_far = lax.ppermute(r_send, ("filt", "space"), crossing(8, 8))
    r_near = lax.ppermute(r_cross, ("filt", "space"), crossing(0, 2))
    c_chip = lax.ppermute(c_here, "space", CORE)
    c_far = lax.ppermute(c_here, ("filt", "space"), BESIDE)

    (mine_y,) = call(code_kernel, [((CODED, 128), BF)], r_keep, r_near, r_far)
    y1, y3, y2 = (lax.ppermute(mine_y, "space", along_y(-r)) for r in (1, 3, 2))
    factor = float((16 * PLANE) ** -0.5)
    (piece,) = call(
        functools.partial(piece_kernel, factor=factor), [((CODED, 128), BF)], mine_y, y1, y2, y3
    )

    (row_bias,) = call(widen_kernel, [((1, OWN), F32)], bias.reshape(1, OWN))
    (wide_bias,) = call(bias_kernel, [((OWN, 1), F32)], row_bias)

    g_mine, g_theirs = call(
        input_grad_kernel,
        [((OWN, PLANE), F32), ((OWN, PLANE + 128), BF)],
        c_chip,
        c_far,
        *cots,
        w_mine,
        w_other,
        scratch=[pltpu.VMEM((9 * 128, PLANE), BF)],
    )
    g_other = lax.ppermute(g_theirs, "filt", ACROSS)
    piece_far = lax.ppermute(piece, "space", XLO)
    got_near = lax.ppermute(piece, "space", CORE)
    got_far = lax.ppermute(piece_far, "space", CORE)
    decoded = [((PIECE, 256), F32)]
    (mine,) = call(decode_kernel, decoded, piece)
    (mine_far,) = call(decode_kernel, decoded, piece_far)
    grad = ((9, 96, 256), F32)
    scratch = [pltpu.VMEM((PIECE, 256), F32), pltpu.SemaphoreType.DMA((5,))]
    hbm = pl.BlockSpec(memory_space=pltpu.HBM)
    half_done, grad_bias, output, grad_inputs = call(
        first_kernel,
        [grad, ((1, OWN), F32), ((OWN, PLANE), F32), ((OWN, PLANE), F32)],
        mine,
        piece,
        got_near,
        o_sum,
        o_got,
        wide_bias,
        g_mine,
        g_other,
        scratch=scratch
        + [pltpu.VMEM(shape, F32) for shape in ((1, OWN), (OWN, PLANE), (OWN, PLANE))]
        + [pltpu.SemaphoreType.DMA((3,))],
        out_space=hbm,
    )
    (grad_weight,) = call(
        second_kernel, [grad], mine_far, got_far, half_done, scratch=scratch, out_space=hbm, over=2
    )
    return (
        output[None],
        grad_inputs[None],
        grad_weight.reshape(3, 3, 3, OWN, 256),
        grad_bias.reshape(OWN),
    )


def solution(mesh):
    placed = (
        P("space", "filt", None),
        P(None, None, None, "filt", None),
        P("filt"),
        P("space", "filt", None),
    )
    return jax.shard_map(
        step,
        mesh=mesh,
        in_specs=placed,
        out_specs=(
            P("space", "filt", None),
            P("space", "filt", None),
            P(None, None, None, "filt", None),
            P("filt"),
        ),
        check_vma=False,
    )
```
